128 devices in a mesh: row: 16 (over y, x_lo, core), col: 8 (over x_hi, z).
Axes of the slice: x: 4 (x_hi: 2, x_lo: 2; x = x_hi * 2 + x_lo), y: 4, z: 4, core: 2. Of those that a mesh axis runs over, the one named last changes fastest.
Arguments:
- tokens: bfloat16 [256, 512, 512], P('row', 'col'), may hold values from -6 to 6
- grad_output: bfloat16 [256, 512, 512], P('row', 'col'), may hold values from -6 to 6
- w_exp: bfloat16 [512, 2048], replicated, may hold values from -0.375 to 0.375
- dw_kernel: float32 [3, 3, 2048], replicated, may hold values from -4.5 to 4.5
- w_proj: bfloat16 [2048, 512], replicated, may hold values from -0.125 to 0.125
- ln_gain: float32 [512], replicated, may hold values from 0.25 to 1.75
- w_qkv: bfloat16 [512, 1536], replicated, may hold values from -16 to 16
- w_out: bfloat16 [512, 512], replicated, may hold values from -0.25 to 0.25
Outputs:
- output: bfloat16 [256, 512, 512], P('row', 'col')
- grad_tokens: bfloat16 [256, 512, 512], P('row', 'col')
The draws below stay inside these ranges and needn't reach their ends.
All inputs are finite; a program needn't handle non-finite values.
Results may differ from the reference program's by a relative error of at most 0.03.
The reference program's roundings to bfloat16 on the way count: a program that leaves them out, or rounds other values in their place, can miss the bound.
Values may be sent and summed in bfloat16 or wider, within the bound.
No kernel may reach another device: no remote copies, remote signals or barrier semaphores. Data moves between devices by JAX's collectives and lax.ppermute only.
A program may use at most 128 MiB of HBM per device.

```python
import jax
import jax.numpy as jnp
from jax import lax

C = 512
HEADS = 16
HD = 32
EXP = 2048
H = 256
W = 512


def draw_w_qkv(key, part):
    draw_base = jax.random.truncated_normal(key, -6.0, 6.0, (C, 3 * C), jnp.float32) * C ** (-0.5)
    return draw_base.astype(jnp.bfloat16)


def block_levels(key, shape, split, least, top_value):
    gain = 1.0
    for dim, parts in split:
        steps = jax.random.uniform(jax.random.fold_in(jax.random.fold_in(key, 6), dim), (parts,), jnp.float32, least / len(split), top_value / len(split))
        gain = gain * jnp.repeat(jnp.exp(steps), shape[dim] // parts).reshape((-1,) + (1,) * (len(shape) - 1 - dim))
    return gain


def noise(stream_key, dims, scale, limit, split=(), kind=jnp.bfloat16):
    result = scale * jax.random.normal(stream_key, dims, jnp.float32)
    if split:
        result = result * block_levels(stream_key, dims, split, -0.22, 0.18)
    return jnp.clip(result, -limit, limit).astype(kind)


def setup_inputs(seed: int = 0) -> dict:
    splits = jax.random.split(jax.random.key(seed), 9)
    return {
        "tokens": noise(splits[0], (H, W, C), 1.0, 6.0, ((0, 16), (1, 8))),
        "grad_output": noise(splits[1], (H, W, C), 1.0, 6.0, ((0, 16), (1, 8))),
        "w_exp": noise(splits[2], (C, EXP), (C // 2) ** -0.5, 0.375),
        "dw_kernel": noise(splits[3], (3, 3, EXP), 1.5, 4.5, (), jnp.float32),
        "w_proj": noise(splits[4], (EXP, C), EXP ** -0.5, 0.125),
        "ln_gain": jnp.clip(1.0 + 0.15 * jax.random.normal(splits[5], (C,), jnp.float32), 0.25, 1.75),
        "w_qkv": draw_w_qkv(jax.random.fold_in(splits[8], 71), 0),
        "w_out": noise(splits[7], (C, C), C ** -0.5, 0.25),
    }


root_two_pi = 0.7978845608028654
cubic_term = 0.044715
epsilon = 1e-05
band_rows = 8

def gelu_tanh(value_in):
    return 0.5 * value_in * (1.0 + jnp.tanh(root_two_pi * (value_in + cubic_term * value_in * value_in * value_in)))

def gelu_slope(value_in):
    tangent = jnp.tanh(root_two_pi * (value_in + cubic_term * value_in * value_in * value_in))
    return 0.5 * (1.0 + tangent) + 0.5 * value_in * (1.0 - tangent * tangent) * root_two_pi * (1.0 + 3.0 * cubic_term * value_in * value_in)

def depthwise(padded, kernel, out_rows, out_cols):
    summed = jnp.zeros((out_rows, out_cols, padded.shape[2]), jnp.float32)
    for row_off in range(3):
        for col_off in range(3):
            summed = summed + padded[row_off:row_off + out_rows, col_off:col_off + out_cols].astype(jnp.float32) * kernel[row_off, col_off]
    return summed

def depthwise_back(padded, kernel, out_rows, out_cols):
    summed = jnp.zeros((out_rows, out_cols, padded.shape[2]), jnp.float32)
    for row_off in range(3):
        for col_off in range(3):
            summed = summed + padded[2 - row_off:2 - row_off + out_rows, 2 - col_off:2 - col_off + out_cols].astype(jnp.float32) * kernel[row_off, col_off]
    return summed

def rounded(array):
    return lax.optimization_barrier(array.astype(jnp.bfloat16)).astype(jnp.float32)

def attend(hidden_win, grad_win, ln_gain, w_qkv, w_out):
    windows, members, width = hidden_win.shape
    hidden_f = hidden_win.astype(jnp.float32)
    center = hidden_f - lax.optimization_barrier(jnp.mean(hidden_f, axis=-1, keepdims=True))
    inv_std = lax.rsqrt(lax.optimization_barrier(jnp.mean(center * center, axis=-1, keepdims=True)) + epsilon)
    unit_norm = center * inv_std
    normed = (unit_norm * ln_gain).astype(jnp.bfloat16)
    packed = jnp.dot(normed.reshape(-1, width), w_qkv, preferred_element_type=jnp.float32)
    packed = rounded(packed).reshape(windows, members, 3, HEADS, HD)
    queries = packed[:, :, 0]
    key_rows = packed[:, :, 1]
    value_rows = packed[:, :, 2]
    score_scale = HD ** (-0.5)
    scores = jnp.einsum('wqhd,wkhd->whqk', queries, key_rows) * score_scale
    row_max = lax.optimization_barrier(jnp.max(scores, axis=-1, keepdims=True))
    lifted = jnp.exp(scores - row_max)
    attn_prob = lifted / lax.optimization_barrier(jnp.sum(lifted, axis=-1, keepdims=True))
    prob_round = rounded(attn_prob)
    attended = jnp.einsum('whqk,wkhd->wqhd', prob_round, value_rows).astype(jnp.bfloat16)
    attn = jnp.dot(attended.reshape(-1, width), w_out, preferred_element_type=jnp.float32).astype(jnp.bfloat16)
    grad_att = jnp.dot(grad_win.reshape(-1, width), w_out.T, preferred_element_type=jnp.float32)
    grad_att = rounded(grad_att).reshape(windows, members, HEADS, HD)
    grad_prob = jnp.einsum('wqhd,wkhd->whqk', grad_att, value_rows)
    grad_val = jnp.einsum('whqk,wqhd->wkhd', prob_round, grad_att).astype(jnp.bfloat16)
    grad_score = attn_prob * (grad_prob - lax.optimization_barrier(jnp.sum(grad_prob * attn_prob, axis=-1, keepdims=True))) * score_scale
    grad_score = rounded(grad_score)
    grad_query = jnp.einsum('whqk,wkhd->wqhd', grad_score, key_rows).astype(jnp.bfloat16)
    grad_key = jnp.einsum('whqk,wqhd->wkhd', grad_score, queries).astype(jnp.bfloat16)
    grad_pack = jnp.stack([grad_query, grad_key, grad_val], axis=2).reshape(-1, 3 * width)
    grad_norm = jnp.dot(grad_pack, w_qkv.T, preferred_element_type=jnp.float32)
    scaled = grad_norm.reshape(windows, members, width) * ln_gain
    grad_attn = inv_std * (scaled - lax.optimization_barrier(jnp.mean(scaled, axis=-1, keepdims=True)) - unit_norm * lax.optimization_barrier(jnp.mean(scaled * unit_norm, axis=-1, keepdims=True)))
    return (attn.reshape(windows, members, width), grad_attn.astype(jnp.bfloat16))

def reference(tokens, grad_output, w_exp, dw_kernel, w_proj, ln_gain, w_qkv, w_out):
    height, breadth, width = tokens.shape
    expand = w_exp.shape[1]
    tok_pad = jnp.pad(tokens, ((2, 2), (2, 2), (0, 0)))
    starts = jnp.arange(height // band_rows, dtype=jnp.int32) * band_rows

    def expand_band(start):
        row_block = lax.dynamic_slice_in_dim(tok_pad, start, band_rows + 4, 0)
        pre_pad = jnp.dot(row_block.reshape(-1, width), w_exp, preferred_element_type=jnp.float32).reshape(band_rows + 4, breadth + 4, expand)
        return (row_block, pre_pad, gelu_tanh(pre_pad).astype(jnp.bfloat16))

    def forward_band(start):
        row_block, pre_pad, act_pad = expand_band(start)
        conv_out = depthwise(act_pad[1:-1, 1:-1], dw_kernel, band_rows, breadth)
        gelu_out = gelu_tanh(conv_out).astype(jnp.bfloat16)
        interior = row_block[2:-2, 2:-2].astype(jnp.float32)
        branch = jnp.dot(gelu_out.reshape(-1, expand), w_proj, preferred_element_type=jnp.float32).reshape(band_rows, breadth, width)
        return (interior + branch).astype(jnp.bfloat16)
    hidden = lax.map(forward_band, starts).reshape(height, breadth, width)

    def to_windows(array):
        return array.reshape(8, height // 8, 8, breadth // 8, width).transpose(1, 3, 0, 2, 4).reshape(height // 8, breadth // 8, 64, width)

    def from_windows(array):
        return array.reshape(height // 8, breadth // 8, 8, 8, width).transpose(2, 0, 3, 1, 4).reshape(height, breadth, width)

    def window_row(window_pair):
        return attend(window_pair[0], window_pair[1], ln_gain, w_qkv, w_out)
    attn_win, grad_win = lax.map(window_row, (to_windows(hidden), to_windows(grad_output)))
    attn = from_windows(attn_win)
    grad_attn = from_windows(grad_win)
    output = (hidden.astype(jnp.float32) + attn.astype(jnp.float32)).astype(jnp.bfloat16)
    grad_hidden = grad_output.astype(jnp.float32) + grad_attn.astype(jnp.float32)
    grad_round = grad_hidden.astype(jnp.bfloat16)
    round_pad = jnp.pad(grad_round, ((1, 1), (1, 1), (0, 0)))

    def backward_band(start):
        row_block, pre_pad, act_pad = expand_band(start)
        conv_rim = depthwise(act_pad, dw_kernel, band_rows + 2, breadth + 2)
        grad_block = lax.dynamic_slice_in_dim(round_pad, start, band_rows + 2, 0)
        grad_mix = jnp.dot(grad_block.reshape(-1, width), w_proj.T, preferred_element_type=jnp.float32).reshape(band_rows + 2, breadth + 2, expand)
        grad_mid = (grad_mix * gelu_slope(conv_rim)).astype(jnp.bfloat16)
        grad_act = depthwise_back(grad_mid, dw_kernel, band_rows, breadth)
        grad_pre = (grad_act * gelu_slope(pre_pad[2:-2, 2:-2])).astype(jnp.bfloat16)
        residual = lax.dynamic_slice_in_dim(grad_hidden, start, band_rows, 0)
        branch = jnp.dot(grad_pre.reshape(-1, expand), w_exp.T, preferred_element_type=jnp.float32).reshape(band_rows, breadth, width)
        return (residual + branch).astype(jnp.bfloat16)
    grad_tokens = lax.map(backward_band, starts).reshape(height, breadth, width)
    return (output, grad_tokens)
```

```python
import functools

import jax
import jax.numpy as jnp
from jax import lax
from jax.experimental import pallas as pl
from jax.experimental.pallas import tpu as pltpu
from jax.sharding import PartitionSpec as P

C0 = 0.7978845608028654
C1 = C0 * 0.044715
BLK = 256
FRAME = 80


def gelu_parts(z):
    z2 = z * z
    t = jnp.tanh(z * (C0 + C1 * z2))
    return z2, t


def gelu_value(z, t):
    half = 0.5 * z
    return half + half * t


def gelu_grad(z, z2, t):
    w = z * (C0 + (3.0 * C1) * z2)
    return (0.5 + 0.5 * t) * (1.0 + (1.0 - t) * w)


def nt(a, b):
    return lax.dot_general(a, b, (((1,), (1,)), ((), ())), preferred_element_type=jnp.float32)


def put_rows(dst, values, row, count, lo, hi):
    for half in range(BLK // 128):
        dst[half, row : row + count, lo:hi, :] = values[:, :, half * 128 : half * 128 + 128]


def conv_row(src, half, row, taps, lo, width, mode):
    if mode == 0:
        total = None
        for a in range(3):
            for b in range(3):
                term = src[half, row + a, lo + b - 1 : lo + b - 1 + width, :] * taps[a][b]
                total = term if total is None else total + term
        return total
    rows = [src[half, row + a] for a in range(3)]
    parts = []
    for b in range(3):
        parts.append(rows[0] * taps[0][b] + rows[1] * taps[1][b] + rows[2] * taps[2][b])
    total = parts[1] + pltpu.roll(parts[0], 1, 0) + pltpu.roll(parts[2], FRAME - 1, 0)
    return total[lo : lo + width]


def read_taps(dw, half, flip):
    grid = []
    for a in range(3):
        line = []
        for b in range(3):
            aa, bb = (2 - a, 2 - b) if flip else (a, b)
            line.append(dw[aa, bb : bb + 1, half * 128 : half * 128 + 128])
        grid.append(line)
    return grid


def fwd_kernel(mode, top, mid, bot, strip, w_exp, dw, w_proj, out, act, acc, gout):
    step = pl.program_id(0)
    width = mid.shape[-1]
    w = w_exp[...]

    def act_of(x, rows, cols):
        z = jnp.dot(x.reshape(rows * cols, width), w, preferred_element_type=jnp.float32)
        _, t = gelu_parts(z)
        a = gelu_value(z, t).astype(jnp.bfloat16).astype(jnp.float32)
        return a.reshape(rows, cols, BLK)

    s = act_of(strip[...], 18, 16)
    put_rows(act, s[:, 0:8], 0, 18, 0, 8)
    put_rows(act, s[:, 8:16], 0, 18, 72, 80)
    put_rows(act, act_of(top[...], 1, 64), 0, 1, 8, 72)
    put_rows(act, act_of(bot[...], 1, 64), 17, 1, 8, 72)
    for r in range(0, 16, 4):
        put_rows(act, act_of(mid[r : r + 4], 4, 64), 1 + r, 4, 8, 72)

    for half in range(BLK // 128):
        taps = read_taps(dw, half, False)
        for r in range(16):
            z = conv_row(act, half, r, taps, 8, 64, mode)
            _, t = gelu_parts(z)
            gout[r * 64 : r * 64 + 64, half * 128 : half * 128 + 128] = gelu_value(z, t).astype(
                jnp.bfloat16
            )
    part = jnp.dot(gout[...], w_proj[...], preferred_element_type=jnp.float32)

    @pl.when(step == 0)
    def _():
        acc[...] = part

    @pl.when(step > 0)
    def _():
        acc[...] += part

    @pl.when(step == pl.num_programs(0) - 1)
    def _():
        out[...] = (mid[...].reshape(1024, width).astype(jnp.float32) + acc[...]).astype(
            jnp.bfloat16
        )


def full(shape):
    return pl.BlockSpec(shape, lambda i: (0,) * len(shape))


def forward(top, mid, bot, strip, w_exp, dw, w_proj, mode=1):
    width, expand = w_exp.shape
    return pl.pallas_call(
        functools.partial(fwd_kernel, mode),
        grid=(expand // BLK,),
        out_shape=jax.ShapeDtypeStruct((1024, width), jnp.bfloat16),
        in_specs=[
            full(top.shape), full(mid.shape), full(bot.shape), full(strip.shape),
            pl.BlockSpec((width, BLK), lambda i: (0, i)),
            pl.BlockSpec((3, 3, BLK), lambda i: (0, 0, i)),
            pl.BlockSpec((BLK, width), lambda i: (i, 0)),
        ],
        out_specs=full((1024, width)),
        scratch_shapes=[
            pltpu.VMEM((BLK // 128, 18, FRAME, 128), jnp.float32),
            pltpu.VMEM((1024, width), jnp.float32),
            pltpu.VMEM((1024, BLK), jnp.bfloat16),
        ],
        name="mbconv_forward",
        compiler_params=pltpu.CompilerParams(vmem_limit_bytes=60 * 1024 * 1024),
    )(top, mid, bot, strip, w_exp, dw, w_proj)


def slope_kernel(mode, top, mid, bot, strip, w_exp, dw, pre_out, conv_out, act):
    width = mid.shape[-1]
    w = w_exp[...]

    def act_of(x, rows, cols, slope_row=None):
        z = jnp.dot(x.reshape(rows * cols, width), w, preferred_element_type=jnp.float32)
        z2, t = gelu_parts(z)
        if slope_row is not None:
            pre_out[slope_row * 64 : (slope_row + rows) * 64, :] = gelu_grad(z, z2, t)
        a = gelu_value(z, t).astype(jnp.bfloat16).astype(jnp.float32)
        return a.reshape(rows, cols, BLK)

    s = act_of(strip[...], 20, 16)
    put_rows(act, s[:, 0:8], 0, 20, 0, 8)
    put_rows(act, s[:, 8:16], 0, 20, 72, 80)
    put_rows(act, act_of(top[...], 2, 64), 0, 2, 8, 72)
    put_rows(act, act_of(bot[...], 2, 64), 18, 2, 8, 72)
    for r in range(0, 16, 4):
        put_rows(act, act_of(mid[r : r + 4], 4, 64, r), 2 + r, 4, 8, 72)

    for half in range(BLK // 128):
        taps = read_taps(dw, half, False)
        for r in range(18):
            z = conv_row(act, half, r, taps, 0, FRAME, 1)
            z2, t = gelu_parts(z)
            conv_out[r * FRAME : r * FRAME + FRAME, half * 128 : half * 128 + 128] = gelu_grad(
                z, z2, t
            )


def slopes(top, mid, bot, strip, w_exp, dw):
    width, expand = w_exp.shape
    return pl.pallas_call(
        functools.partial(slope_kernel, 1),
        grid=(expand // BLK,),
        out_shape=(
            jax.ShapeDtypeStruct((1024, expand), jnp.float32),
            jax.ShapeDtypeStruct((18 * FRAME, expand), jnp.float32),
        ),
        in_specs=[
            full(top.shape), full(mid.shape), full(bot.shape), full(strip.shape),
            pl.BlockSpec((width, BLK), lambda i: (0, i)),
            pl.BlockSpec((3, 3, BLK), lambda i: (0, 0, i)),
        ],
        out_specs=(
            pl.BlockSpec((1024, BLK), lambda i: (0, i)),
            pl.BlockSpec((18 * FRAME, BLK), lambda i: (0, i)),
        ),
        scratch_shapes=[pltpu.VMEM((BLK // 128, 20, FRAME, 128), jnp.float32)],
        name="mbconv_slopes",
        compiler_params=pltpu.CompilerParams(vmem_limit_bytes=60 * 1024 * 1024),
    )(top, mid, bot, strip, w_exp, dw)


def bwd_kernel(top, grad, back, bot, strip, pre_slope, conv_slope, w_exp, dw, w_proj, out,
               mixed, pre, acc):
    step = pl.program_id(0)
    width = grad.shape[-1]
    wp = w_proj[...]

    def mix_of(x):
        return nt(x, wp)

    def slope_at(row, count, lo, hi):
        return conv_slope[...].reshape(18, FRAME, BLK)[row : row + count, lo:hi]

    def put(mix, row, count, lo, hi):
        mid = mix.reshape(count, hi - lo, BLK) * slope_at(row, count, lo, hi)
        put_rows(mixed, mid.astype(jnp.bfloat16).astype(jnp.float32), row, count, lo, hi)

    edge = mix_of(strip[...]).reshape(18, 16, BLK)
    put(edge[:, 0:8], 0, 18, 0, 8)
    put(edge[:, 8:16], 0, 18, 72, 80)
    put(mix_of(top[...]), 0, 1, 8, 72)
    put(mix_of(bot[...]), 17, 1, 8, 72)
    for r in range(0, 16, 4):
        rows = slice(r * 64, r * 64 + 256)
        full_grad = grad[rows].astype(jnp.float32) + back[rows].astype(jnp.float32)
        put(mix_of(full_grad.astype(jnp.bfloat16)), 1 + r, 4, 8, 72)

    for half in range(BLK // 128):
        taps = read_taps(dw, half, True)
        lanes = slice(half * 128, half * 128 + 128)
        for r in range(16):
            z = conv_row(mixed, half, r, taps, 8, 64, 0)
            rows = slice(r * 64, r * 64 + 64)
            pre[rows, lanes] = (z * pre_slope[rows, lanes]).astype(jnp.bfloat16)
    part = nt(pre[...], w_exp[...])

    @pl.when(step == 0)
    def _():
        acc[...] = part

    @pl.when(step > 0)
    def _():
        acc[...] += part

    @pl.when(step == pl.num_programs(0) - 1)
    def _():
        full_grad = grad[...].astype(jnp.float32) + back[...].astype(jnp.float32)
        out[...] = (full_grad + acc[...]).astype(jnp.bfloat16)


def backward(top, grad, back, bot, strip, pre_slope, conv_slope, w_exp, dw, w_proj):
    width, expand = w_exp.shape
    return pl.pallas_call(
        bwd_kernel,
        grid=(expand // BLK,),
        out_shape=jax.ShapeDtypeStruct((1024, width), jnp.bfloat16),
        in_specs=[
            full(top.shape), full(grad.shape), full(back.shape), full(bot.shape),
            full(strip.shape),
            pl.BlockSpec((1024, BLK), lambda i: (0, i)),
            pl.BlockSpec((18 * FRAME, BLK), lambda i: (0, i)),
            pl.BlockSpec((width, BLK), lambda i: (0, i)),
            pl.BlockSpec((3, 3, BLK), lambda i: (0, 0, i)),
            pl.BlockSpec((BLK, width), lambda i: (i, 0)),
        ],
        out_specs=full((1024, width)),
        scratch_shapes=[
            pltpu.VMEM((BLK // 128, 18, FRAME, 128), jnp.float32),
            pltpu.VMEM((1024, BLK), jnp.bfloat16),
            pltpu.VMEM((1024, width), jnp.float32),
        ],
        name="mbconv_backward",
        compiler_params=pltpu.CompilerParams(vmem_limit_bytes=60 * 1024 * 1024),
    )(top, grad, back, bot, strip, pre_slope, conv_slope, w_exp, dw, w_proj)


WINDOWS = 16
GROUP = 4


def gather_window(src, w):
    return jnp.concatenate(
        [src[c, pl.ds(w, 64, stride=WINDOWS), :] for c in range(4)], axis=1
    )


def scatter_window(dst, w, values):
    for c in range(4):
        dst[c, pl.ds(w, 64, stride=WINDOWS), :] = values[:, c * 128 : c * 128 + 128]


def attend_kernel(hid, gatt, gain, w_qkv, back_out, att_out, hs, gs, packed, gpack):
    scale = 32 ** (-0.5)
    for c in range(4):
        hs[c] = hid[:, c * 128 : c * 128 + 128].astype(jnp.float32)
        gs[c] = gatt[:, c * 128 : c * 128 + 128].astype(jnp.float32)
    lane = lax.broadcasted_iota(jnp.int32, (64, 128), 1)
    masks = [(lane >= 32 * h) & (lane < 32 * h + 32) for h in range(4)]
    gain_row = gain[...]

    def spread(x):
        zero = jnp.zeros_like(x)
        return jnp.concatenate([jnp.where(m, x, zero) for m in masks], axis=0)

    def collect(y):
        total = None
        for h in range(4):
            term = jnp.where(masks[h], y[h * 64 : h * 64 + 64], 0.0)
            total = term if total is None else total + term
        return total

    def tn(a, b):
        return lax.dot_general(a, b, (((0,), (0,)), ((), ())), preferred_element_type=jnp.float32)

    def body(group, carry):
        base = group * GROUP
        x = jnp.concatenate([gather_window(hs, base + i) for i in range(GROUP)], axis=0)
        center = x - jnp.mean(x, axis=-1, keepdims=True)
        inv_std = lax.rsqrt(jnp.mean(center * center, axis=-1, keepdims=True) + 1e-5)
        unit = center * inv_std
        normed = (unit * gain_row).astype(jnp.bfloat16)
        packed[...] = jnp.dot(normed, w_qkv[...], preferred_element_type=jnp.float32).astype(
            jnp.bfloat16
        )
        for i in range(GROUP):
            g_all = gather_window(gs, base + i).astype(jnp.bfloat16)
            rows = slice(i * 64, i * 64 + 64)
            outs = []
            for hg in range(4):
                lo = hg * 128
                q = packed[rows, lo : lo + 128]
                k = packed[rows, 512 + lo : 512 + lo + 128]
                v = packed[rows, 1024 + lo : 1024 + lo + 128]
                g = g_all[:, lo : lo + 128]
                q_bd = spread(q)
                g_bd = spread(g)
                s = nt(k, q_bd) * scale
                dp = nt(v, g_bd)
                e = jnp.exp(s - jnp.max(s, axis=0, keepdims=True))
                p = e * (1.0 / jnp.sum(e, axis=0, keepdims=True))
                p_bf = p.astype(jnp.bfloat16)
                dot = jnp.sum(dp * p, axis=0, keepdims=True)
                ds = (p * (dp - dot) * scale).astype(jnp.bfloat16)
                dv = jnp.dot(p_bf, g_bd, preferred_element_type=jnp.float32)
                dk = jnp.dot(ds, q_bd, preferred_element_type=jnp.float32)
                dq = collect(tn(ds, k))
                outs.append(collect(tn(p_bf, v)))
                gpack[rows, lo : lo + 128] = dq.astype(jnp.bfloat16)
                gpack[rows, 512 + lo : 512 + lo + 128] = dk.astype(jnp.bfloat16)
                gpack[rows, 1024 + lo : 1024 + lo + 128] = dv.astype(jnp.bfloat16)
            scatter_window(gs, base + i, jnp.concatenate(outs, axis=1))
        scaled = nt(gpack[...], w_qkv[...]) * gain_row
        grad = inv_std * (
            scaled
            - jnp.mean(scaled, axis=-1, keepdims=True)
            - unit * jnp.mean(scaled * unit, axis=-1, keepdims=True)
        )
        for i in range(GROUP):
            scatter_window(hs, base + i, grad[i * 64 : i * 64 + 64])
        return carry

    lax.fori_loop(0, WINDOWS // GROUP, body, 0)
    for c in range(4):
        back_out[:, c * 128 : c * 128 + 128] = hs[c].astype(jnp.bfloat16)
        att_out[:, c * 128 : c * 128 + 128] = gs[c].astype(jnp.bfloat16)


def attend(hid, gatt, gain, w_qkv):
    vm = pl.BlockSpec(memory_space=pltpu.VMEM)
    return pl.pallas_call(
        attend_kernel,
        out_shape=(jax.ShapeDtypeStruct(hid.shape, jnp.bfloat16),) * 2,
        in_specs=[vm] * 4,
        out_specs=(vm, vm),
        scratch_shapes=[
            pltpu.VMEM((4, 1024, 128), jnp.float32),
            pltpu.VMEM((4, 1024, 128), jnp.float32),
            pltpu.VMEM((GROUP * 64, 1536), jnp.bfloat16),
            pltpu.VMEM((GROUP * 64, 1536), jnp.bfloat16),
        ],
        name="window_attention",
        compiler_params=pltpu.CompilerParams(vmem_limit_bytes=48 * 1024 * 1024),
    )(hid, gatt, gain, w_qkv)


def neighbour_pair(axis, size, to_next, to_prev):
    up = [(i, i + 1) for i in range(size - 1)]
    down = [(i + 1, i) for i in range(size - 1)]
    return lax.ppermute(to_next, axis, up), lax.ppermute(to_prev, axis, down)


def edge_strip(left, right, halo):
    gap = jnp.zeros((left.shape[0], 8 - halo, left.shape[2]), left.dtype)
    return jnp.concatenate([gap, left, right, gap], axis=1)


def per_device(tokens, grad_output, w_exp, dw_kernel, w_proj, ln_gain, w_qkv, w_out):
    rows, cols, width = tokens.shape
    row_count = lax.axis_size("row")
    col_count = lax.axis_size("col")
    peers = row_count * col_count // 2
    groups = [
        [(2 * q + h) * col_count + c for q in range(row_count // 2) for c in range(col_count)]
        for h in range(2)
    ]
    axes = ("row", "col")

    def exchange(flat):
        blocks = flat.reshape(peers, rows * cols // peers, width)
        moved = lax.all_to_all(
            blocks, axes, split_axis=0, concat_axis=0, tiled=True, axis_index_groups=groups
        )
        return moved.reshape(rows * cols, width)

    top, bot = neighbour_pair("row", row_count, tokens[rows - 2 :], tokens[:2])
    grad_flat = grad_output.reshape(rows * cols, width)
    grad_att = jnp.dot(grad_flat, w_out.T, preferred_element_type=jnp.float32).astype(jnp.bfloat16)
    grad_win = exchange(grad_att)

    to_right = jnp.concatenate([top[:, cols - 2 :], tokens[:, cols - 2 :], bot[:, cols - 2 :]], 0)
    to_left = jnp.concatenate([top[:, :2], tokens[:, :2], bot[:, :2]], 0)
    left, right = neighbour_pair("col", col_count, to_right, to_left)
    strip = edge_strip(left, right, 2)

    hidden = forward(
        top[1:], tokens, bot[:1], strip[1:-1], w_exp, dw_kernel, w_proj, mode=0
    )
    hidden, grad_win = lax.optimization_barrier((hidden, grad_win))
    hidden_win = exchange(hidden)
    w_late, _ = lax.optimization_barrier((w_exp, hidden))
    pre_slope, conv_slope = slopes(top, tokens, bot, strip, w_late, dw_kernel)
    hidden_win, pre_slope, conv_slope = lax.optimization_barrier(
        (hidden_win, pre_slope, conv_slope)
    )
    back_win, att_win = attend(hidden_win, grad_win, ln_gain.reshape(1, width), w_qkv)
    back = exchange(back_win)
    attn_win = jnp.dot(att_win, w_out, preferred_element_type=jnp.float32).astype(jnp.bfloat16)
    attn = exchange(attn_win)

    def rounded_at(row_slice, col_slice):
        one = grad_output[row_slice, col_slice].astype(jnp.float32)
        two = back.reshape(rows, cols, width)[row_slice, col_slice].astype(jnp.float32)
        return (one + two).astype(jnp.bfloat16)

    every = slice(None)
    g_top, g_bot = neighbour_pair(
        "row", row_count, rounded_at(slice(rows - 1, rows), every), rounded_at(slice(0, 1), every)
    )

    def grad_column(lo):
        at = slice(lo, lo + 1)
        return jnp.concatenate([g_top[:, at], rounded_at(every, at), g_bot[:, at]], axis=0)

    g_left, g_right = neighbour_pair("col", col_count, grad_column(cols - 1), grad_column(0))
    g_strip = edge_strip(g_left, g_right, 1)
    grad_tokens = backward(
        g_top.reshape(cols, width), grad_flat, back, g_bot.reshape(cols, width),
        g_strip.reshape(-1, width), pre_slope, conv_slope, w_exp, dw_kernel, w_proj,
    )
    output = (hidden.astype(jnp.float32) + attn.astype(jnp.float32)).astype(jnp.bfloat16)
    return output.reshape(tokens.shape), grad_tokens.reshape(tokens.shape)


def solution(mesh):
    in_specs = (P("row", "col", None), P("row", "col", None), P(), P(), P(), P(), P(), P())
    out_specs = (P("row", "col", None), P("row", "col", None))
    return jax.shard_map(
        per_device, mesh=mesh, in_specs=in_specs, out_specs=out_specs, check_vma=False
    )
```

```python
import functools

import jax
import jax.numpy as jnp
from jax import lax
from jax.experimental import pallas as pl
from jax.experimental.pallas import tpu as pltpu
from jax.sharding import PartitionSpec as P

C0 = 0.7978845608028654
C1 = C0 * 0.044715
BLK = 256
FRAME = 80
EDGE = 24
LIMIT = 60 * 1024 * 1024


def half_gelu(h):
    h2 = h * h
    return h2, jnp.tanh(h * ((2.0 * C0) + (8.0 * C1) * h2))


def gelu_value(h, t):
    return h + h * t


def double_slope(h, h2, t):
    return (1.0 + t) + (1.0 - t * t) * (h * ((2.0 * C0) + (24.0 * C1) * h2))


def nt(a, b):
    return lax.dot_general(a, b, (((1,), (1,)), ((), ())), preferred_element_type=jnp.float32)


def round_f32(x):
    return x.astype(jnp.bfloat16).astype(jnp.float32)


def lanes_of(part):
    return slice(part * 128, part * 128 + 128)


def put_rows(dst, values, row, count):
    for part in range(BLK // 128):
        dst[part, row : row + count, 8:72, :] = values[:, lanes_of(part)].reshape(count, 64, 128)


def put_edge(dst, values, first, count, col):
    for part in range(BLK // 128):
        for r in range(count):
            dst[part, r, col : col + 1, :] = values[first + r : first + r + 1, lanes_of(part)]


def conv_row(src, part, row, taps):
    total = None
    for a in range(3):
        for b in range(3):
            term = src[part, row + a, 7 + b : 71 + b, :] * taps[a][b]
            total = term if total is None else total + term
    return total


def read_taps(dw, part, flip):
    taps = []
    for a in range(3):
        aa = 2 - a if flip else a
        order = (2, 1, 0) if flip else (0, 1, 2)
        taps.append([0.5 * dw[aa, b : b + 1, lanes_of(part)] for b in order])
    return taps


def fwd_kernel(top, mid, bot, left, right, w_exp, dw, w_proj, out, act, acc, gout):
    step = pl.program_id(0)
    width = mid.shape[-1]
    w = w_exp[...] * jnp.bfloat16(0.5)

    @pl.when(step == 0)
    def _():
        acc[...] = mid[...].reshape(1024, width).astype(jnp.float32)

    def act_of(x):
        h = jnp.dot(x, w, preferred_element_type=jnp.float32)
        _, t = half_gelu(h)
        return round_f32(gelu_value(h, t))

    put_edge(act, act_of(left[...])[EDGE:], 1, 18, 7)
    put_edge(act, act_of(right[...])[:EDGE], 1, 18, 72)
    put_rows(act, act_of(top[1]), 0, 1)
    for r in range(0, 16, 4):
        put_rows(act, act_of(mid[r : r + 4].reshape(256, width)), 1 + r, 4)
    put_rows(act, act_of(bot[0]), 17, 1)

    for part in range(BLK // 128):
        taps = read_taps(dw, part, False)
        for r in range(16):
            h = conv_row(act, part, r, taps)
            _, t = half_gelu(h)
            gout[r * 64 : r * 64 + 64, lanes_of(part)] = gelu_value(h, t).astype(jnp.bfloat16)
    wp = w_proj[...]
    for r in range(0, 1024, 256):
        acc[r : r + 256] += jnp.dot(gout[r : r + 256], wp, preferred_element_type=jnp.float32)

    @pl.when(step == pl.num_programs(0) - 1)
    def _():
        out[...] = acc[...].astype(jnp.bfloat16)


def full(shape):
    return pl.BlockSpec(shape, lambda i: (0,) * len(shape))


def forward(top, mid, bot, left, right, w_exp, dw, w_proj):
    width, expand = w_exp.shape
    return pl.pallas_call(
        fwd_kernel,
        grid=(expand // BLK,),
        out_shape=jax.ShapeDtypeStruct((1024, width), jnp.bfloat16),
        in_specs=[
            full(top.shape), full(mid.shape), full(bot.shape), full(left.shape),
            full(right.shape),
            pl.BlockSpec((width, BLK), lambda i: (0, i)),
            pl.BlockSpec((3, 3, BLK), lambda i: (0, 0, i)),
            pl.BlockSpec((BLK, width), lambda i: (i, 0)),
        ],
        out_specs=full((1024, width)),
        scratch_shapes=[
            pltpu.VMEM((BLK // 128, 18, FRAME, 128), jnp.float32),
            pltpu.VMEM((1024, width), jnp.float32),
            pltpu.VMEM((1024, BLK), jnp.bfloat16),
        ],
        name="mbconv_forward",
        compiler_params=pltpu.CompilerParams(vmem_limit_bytes=LIMIT),
    )(top, mid, bot, left, right, w_exp, dw, w_proj)


def slope_kernel(top, mid, bot, left, near_left, near_right, right, w_exp, dw,
                 pre_out, conv_out, edge_out, act, cols):
    width = mid.shape[-1]
    w = w_exp[...] * jnp.bfloat16(0.5)

    def act_of(x, slope_row=None):
        h = jnp.dot(x, w, preferred_element_type=jnp.float32)
        h2, t = half_gelu(h)
        if slope_row is not None:
            pre_out[slope_row * 64 : slope_row * 64 + x.shape[0], :] = double_slope(h, h2, t)
        return round_f32(gelu_value(h, t))

    for side, pair in enumerate((left, near_left, near_right, right)):
        a = act_of(pair[...])
        for part in range(BLK // 128):
            cols[part, 2 * side : 2 * side + 2, :, :] = a[:, lanes_of(part)].reshape(2, EDGE, 128)
        if side == 0:
            put_edge(act, a[EDGE:], 0, 20, 7)
        if side == 3:
            put_edge(act, a[:EDGE], 0, 20, 72)
    put_rows(act, act_of(top[...].reshape(128, width)), 0, 2)
    for r in range(0, 16, 4):
        put_rows(act, act_of(mid[r : r + 4].reshape(256, width), r), 2 + r, 4)
    put_rows(act, act_of(bot[...].reshape(128, width)), 18, 2)

    for part in range(BLK // 128):
        taps = read_taps(dw, part, False)
        for r in range(18):
            h = conv_row(act, part, r, taps)
            h2, t = half_gelu(h)
            conv_out[r * 64 : r * 64 + 64, lanes_of(part)] = double_slope(h, h2, t)
        for side in range(2):
            h = None
            for a in range(3):
                for b in range(3):
                    term = cols[part, 5 * side + b, a : a + 18, :] * taps[a][b]
                    h = term if h is None else h + term
            h2, t = half_gelu(h)
            edge_out[side * EDGE : side * EDGE + 18, lanes_of(part)] = double_slope(h, h2, t)
            edge_out[side * EDGE + 18 : side * EDGE + EDGE, lanes_of(part)] = jnp.zeros(
                (EDGE - 18, 128), jnp.float32
            )


def slopes(top, mid, bot, left, near_left, near_right, right, w_exp, dw, first, count):
    width = w_exp.shape[0]
    side = full(left.shape)
    rows = (1024, 18 * 64, 2 * EDGE)
    return pl.pallas_call(
        slope_kernel,
        grid=(count,),
        out_shape=tuple(jax.ShapeDtypeStruct((n, count * BLK), jnp.float32) for n in rows),
        in_specs=[
            full(top.shape), full(mid.shape), full(bot.shape), side, side, side, side,
            pl.BlockSpec((width, BLK), lambda i: (0, i + first)),
            pl.BlockSpec((3, 3, BLK), lambda i: (0, 0, i + first)),
        ],
        out_specs=tuple(pl.BlockSpec((n, BLK), lambda i: (0, i)) for n in rows),
        scratch_shapes=[
            pltpu.VMEM((BLK // 128, 20, FRAME, 128), jnp.float32),
            pltpu.VMEM((BLK // 128, 8, EDGE, 128), jnp.float32),
        ],
        name="mbconv_slopes",
        compiler_params=pltpu.CompilerParams(vmem_limit_bytes=LIMIT),
    )(top, mid, bot, left, near_left, near_right, right, w_exp, dw)


def bwd_kernel(split, top, grad, back, bot, left, right, *rest):
    tables, (w_exp, dw, w_proj, out, mixed, pre, acc, rounded) = rest[:6], rest[6:]
    step = pl.program_id(0)

    @pl.when(step == 0)
    def _():
        total = grad[...].astype(jnp.float32) + back[...].astype(jnp.float32)
        acc[...] = total
        rounded[...] = total.astype(jnp.bfloat16)

    def work(pre_slope, conv_slope, edge_slope):
        wp = w_proj[...] * jnp.bfloat16(0.5)
        for side, col in ((left, 7), (right, 72)):
            at = 0 if col == 7 else EDGE
            put_edge(
                mixed, round_f32(nt(side[...], wp) * edge_slope[at : at + EDGE]), 0, 18, col
            )

        def put(x, row, count):
            mid = nt(x, wp) * conv_slope[row * 64 : (row + count) * 64]
            put_rows(mixed, round_f32(mid), row, count)

        put(top[...], 0, 1)
        for r in range(0, 16, 4):
            put(rounded[r * 64 : r * 64 + 256], 1 + r, 4)
        put(bot[...], 17, 1)

        for part in range(BLK // 128):
            taps = read_taps(dw, part, True)
            for r in range(16):
                rows = slice(r * 64, r * 64 + 64)
                z = conv_row(mixed, part, r, taps) * pre_slope[rows, lanes_of(part)]
                pre[rows, lanes_of(part)] = z.astype(jnp.bfloat16)
        w = w_exp[...]
        for r in range(0, 1024, 256):
            acc[r : r + 256] += nt(pre[r : r + 256], w)

    @pl.when(step < split)
    def _():
        work(*tables[:3])

    @pl.when(step >= split)
    def _():
        work(*tables[3:])

    @pl.when(step == pl.num_programs(0) - 1)
    def _():
        out[...] = acc[...].astype(jnp.bfloat16)


def backward(top, grad, back, bot, left, right, early, late, w_exp, dw, w_proj):
    width, expand = w_exp.shape
    split = early[0].shape[1] // BLK
    return pl.pallas_call(
        functools.partial(bwd_kernel, split),
        grid=(expand // BLK,),
        out_shape=jax.ShapeDtypeStruct((1024, width), jnp.bfloat16),
        in_specs=[
            full(top.shape), full(grad.shape), full(back.shape), full(bot.shape),
            full(left.shape), full(right.shape),
            *(pl.BlockSpec((x.shape[0], BLK), lambda i: (0, jnp.minimum(i, split - 1)))
              for x in early),
            *(pl.BlockSpec((x.shape[0], BLK), lambda i: (0, jnp.maximum(i - split, 0)))
              for x in late),
            pl.BlockSpec((width, BLK), lambda i: (0, i)),
            pl.BlockSpec((3, 3, BLK), lambda i: (0, 0, i)),
            pl.BlockSpec((BLK, width), lambda i: (i, 0)),
        ],
        out_specs=full((1024, width)),
        scratch_shapes=[
            pltpu.VMEM((BLK // 128, 18, FRAME, 128), jnp.float32),
            pltpu.VMEM((1024, BLK), jnp.bfloat16),
            pltpu.VMEM((1024, width), jnp.float32),
            pltpu.VMEM((1024, width), jnp.bfloat16),
        ],
        name="mbconv_backward",
        compiler_params=pltpu.CompilerParams(vmem_limit_bytes=LIMIT),
    )(top, grad, back, bot, left, right, *early, *late, w_exp, dw, w_proj)


WINDOWS = 16
GROUP = 4
BREADTH = 2
FLAGS = None


def gather_window(src, w):
    return jnp.concatenate(
        [src[c, pl.ds(w, 64, stride=WINDOWS), :] for c in range(4)], axis=1
    )


def scatter_window(dst, w, values):
    for c in range(4):
        dst[c, pl.ds(w, 64, stride=WINDOWS), :] = values[:, c * 128 : c * 128 + 128]


def attend_kernel(hid, gatt, gain, w_qkv, back_out, att_out, hs, gs, packed, gpack):
    scale = 32 ** (-0.5)
    for c in range(4):
        hs[c] = hid[:, c * 128 : c * 128 + 128].astype(jnp.float32)
        gs[c] = gatt[:, c * 128 : c * 128 + 128].astype(jnp.float32)
    lane = lax.broadcasted_iota(jnp.int32, (64, 128), 1)
    masks = [(lane >= 32 * h) & (lane < 32 * h + 32) for h in range(4)]
    gain_row = gain[...]

    def spread(x):
        zero = jnp.zeros_like(x)
        return jnp.concatenate([jnp.where(m, x, zero) for m in masks], axis=0)

    def collect(y):
        total = None
        for h in range(4):
            term = jnp.where(masks[h], y[h * 64 : h * 64 + 64], 0.0)
            total = term if total is None else total + term
        return total

    def tn(a, b):
        return lax.dot_general(a, b, (((0,), (0,)), ((), ())), preferred_element_type=jnp.float32)

    def body(group, carry):
        base = group * GROUP
        x = jnp.concatenate([gather_window(hs, base + i) for i in range(GROUP)], axis=0)
        center = x - jnp.mean(x, axis=-1, keepdims=True)
        inv_std = lax.rsqrt(jnp.mean(center * center, axis=-1, keepdims=True) + 1e-5)
        unit = center * inv_std
        normed = (unit * gain_row).astype(jnp.bfloat16)
        packed[...] = jnp.dot(normed, w_qkv[...], preferred_element_type=jnp.float32).astype(
            jnp.bfloat16
        )
        units = [(i, hg) for i in range(GROUP) for hg in range(4)]
        g_all = [gather_window(gs, base + i).astype(jnp.bfloat16) for i in range(GROUP)]
        outs = {}
        for first in range(0, len(units), BREADTH):
            batch = units[first : first + BREADTH]
            st = []
            for i, hg in batch:
                rows = slice(i * 64, i * 64 + 64)
                lo = hg * 128
                k = packed[rows, 512 + lo : 512 + lo + 128]
                v = packed[rows, 1024 + lo : 1024 + lo + 128]
                q_bd = spread(packed[rows, lo : lo + 128])
                g_bd = spread(g_all[i][:, lo : lo + 128])
                st.append((k, v, q_bd, g_bd))
            sd = [(nt(k, q_bd), nt(v, g_bd)) for k, v, q_bd, g_bd in st]
            soft = []
            for s, dp in sd:
                s = s * scale
                e = jnp.exp(s - jnp.max(s, axis=0, keepdims=True))
                p = e * (1.0 / jnp.sum(e, axis=0, keepdims=True))
                dot = jnp.sum(dp * p, axis=0, keepdims=True)
                soft.append((p.astype(jnp.bfloat16), (p * (dp - dot) * scale).astype(jnp.bfloat16)))
            prods = []
            for (k, v, q_bd, g_bd), (p, ds) in zip(st, soft):
                prods.append((
                    jnp.dot(p, g_bd, preferred_element_type=jnp.float32),
                    jnp.dot(ds, q_bd, preferred_element_type=jnp.float32),
                    tn(ds, k),
                    tn(p, v),
                ))
            for (i, hg), (dv, dk, dq, o) in zip(batch, prods):
                rows = slice(i * 64, i * 64 + 64)
                lo = hg * 128
                gpack[rows, lo : lo + 128] = collect(dq).astype(jnp.bfloat16)
                gpack[rows, 512 + lo : 512 + lo + 128] = dk.astype(jnp.bfloat16)
                gpack[rows, 1024 + lo : 1024 + lo + 128] = dv.astype(jnp.bfloat16)
                outs[i, hg] = collect(o)
        for i in range(GROUP):
            scatter_window(gs, base + i, jnp.concatenate([outs[i, hg] for hg in range(4)], axis=1))
        scaled = nt(gpack[...], w_qkv[...]) * gain_row
        grad = inv_std * (
            scaled
            - jnp.mean(scaled, axis=-1, keepdims=True)
            - unit * jnp.mean(scaled * unit, axis=-1, keepdims=True)
        )
        for i in range(GROUP):
            scatter_window(hs, base + i, grad[i * 64 : i * 64 + 64])
        return carry

    lax.fori_loop(0, WINDOWS // GROUP, body, 0)
    for c in range(4):
        back_out[:, c * 128 : c * 128 + 128] = hs[c].astype(jnp.bfloat16)
        att_out[:, c * 128 : c * 128 + 128] = gs[c].astype(jnp.bfloat16)


def attend(hid, gatt, gain, w_qkv):
    vm = pl.BlockSpec(memory_space=pltpu.VMEM)
    return pl.pallas_call(
        attend_kernel,
        out_shape=(jax.ShapeDtypeStruct(hid.shape, jnp.bfloat16),) * 2,
        in_specs=[vm] * 4,
        out_specs=(vm, vm),
        scratch_shapes=[
            pltpu.VMEM((4, 1024, 128), jnp.float32),
            pltpu.VMEM((4, 1024, 128), jnp.float32),
            pltpu.VMEM((GROUP * 64, 1536), jnp.bfloat16),
            pltpu.VMEM((GROUP * 64, 1536), jnp.bfloat16),
        ],
        name="window_attention",
        compiler_params=pltpu.CompilerParams(vmem_limit_bytes=48 * 1024 * 1024, flags=FLAGS),
    )(hid, gatt, gain, w_qkv)


def neighbour_pair(axis, size, to_next, to_prev):
    up = [(i, i + 1) for i in range(size - 1)]
    down = [(i + 1, i) for i in range(size - 1)]
    return lax.ppermute(to_next, axis, up), lax.ppermute(to_prev, axis, down)


def edge_columns(parts):
    rows = jnp.concatenate(parts, axis=0).transpose(1, 0, 2)
    rows = jnp.pad(rows, ((0, 0), (0, EDGE - rows.shape[1]), (0, 0)))
    return rows.reshape(-1, rows.shape[2])


EARLY = 5


def per_device(tokens, grad_output, w_exp, dw_kernel, w_proj, ln_gain, w_qkv, w_out):
    rows, cols, width = tokens.shape
    blocks = w_exp.shape[1] // BLK
    row_count = lax.axis_size("row")
    col_count = lax.axis_size("col")
    peers = row_count * col_count // 2
    groups = [
        [(2 * q + h) * col_count + c for q in range(row_count // 2) for c in range(col_count)]
        for h in range(2)
    ]
    axes = ("row", "col")

    def exchange(flat):
        sent = flat.reshape(peers, rows * cols // peers, width)
        moved = lax.all_to_all(
            sent, axes, split_axis=0, concat_axis=0, tiled=True, axis_index_groups=groups
        )
        return moved.reshape(rows * cols, width)

    top, bot = neighbour_pair("row", row_count, tokens[rows - 2 :], tokens[:2])
    grad_flat = grad_output.reshape(rows * cols, width)
    grad_att = jnp.dot(grad_flat, w_out.T, preferred_element_type=jnp.float32).astype(jnp.bfloat16)
    grad_win = exchange(grad_att)

    near_right = edge_columns([x[:, cols - 2 :] for x in (top, tokens, bot)])
    near_left = edge_columns([x[:, :2] for x in (top, tokens, bot)])
    left, right = neighbour_pair("col", col_count, near_right, near_left)

    hidden = forward(top, tokens, bot, left, right, w_exp, dw_kernel, w_proj)
    hidden, grad_win = lax.optimization_barrier((hidden, grad_win))
    hidden_win = exchange(hidden)
    w_late, _ = lax.optimization_barrier((w_exp, hidden))
    halo = (top, tokens, bot, left, near_left, near_right, right)
    early = slopes(*halo, w_late, dw_kernel, 0, EARLY)
    hidden_win, *early = lax.optimization_barrier((hidden_win, *early))
    back_win, att_win = attend(hidden_win, grad_win, ln_gain.reshape(1, width), w_qkv)
    back = exchange(back_win)
    w_last, att_win = lax.optimization_barrier((w_exp, att_win))
    late = slopes(*halo, w_last, dw_kernel, EARLY, blocks - EARLY)
    attn_win = jnp.dot(att_win, w_out, preferred_element_type=jnp.float32).astype(jnp.bfloat16)
    back, attn_win, *late = lax.optimization_barrier((back, attn_win, *late))
    attn = exchange(attn_win)

    def rounded_at(row_slice, col_slice):
        one = grad_output[row_slice, col_slice].astype(jnp.float32)
        two = back.reshape(rows, cols, width)[row_slice, col_slice].astype(jnp.float32)
        return (one + two).astype(jnp.bfloat16)

    every = slice(None)
    g_top, g_bot = neighbour_pair(
        "row", row_count, rounded_at(slice(rows - 1, rows), every), rounded_at(slice(0, 1), every)
    )

    def grad_column(lo):
        at = slice(lo, lo + 1)
        return edge_columns([g_top[:, at], rounded_at(every, at), g_bot[:, at]])

    g_left, g_right = neighbour_pair("col", col_count, grad_column(cols - 1), grad_column(0))
    grad_tokens = backward(
        g_top.reshape(cols, width), grad_flat, back, g_bot.reshape(cols, width),
        g_left, g_right, early, late, w_exp, dw_kernel, w_proj,
    )
    output = (hidden.astype(jnp.float32) + attn.astype(jnp.float32)).astype(jnp.bfloat16)
    return output.reshape(tokens.shape), grad_tokens.reshape(tokens.shape)


def solution(mesh):
    in_specs = (P("row", "col", None), P("row", "col", None), P(), P(), P(), P(), P(), P())
    out_specs = (P("row", "col", None), P("row", "col", None))
    return jax.shard_map(
        per_device, mesh=mesh, in_specs=in_specs, out_specs=out_specs, check_vma=False
    )
```

```python
import functools

import jax
import jax.numpy as jnp
from jax import lax
from jax.experimental import pallas as pl
from jax.experimental.pallas import tpu as pltpu
from jax.sharding import PartitionSpec as P

C0 = 0.7978845608028654
C1 = C0 * 0.044715
BLK = 256
FRAME = 80
EDGE = 24
LIMIT = 60 * 1024 * 1024


def half_gelu(h):
    h2 = h * h
    return h2, jnp.tanh(h * ((2.0 * C0) + (8.0 * C1) * h2))


def gelu_value(h, t):
    return h + h * t


def double_slope(h, h2, t):
    return (1.0 + t) + (1.0 - t * t) * (h * ((2.0 * C0) + (24.0 * C1) * h2))


def nt(a, b):
    return lax.dot_general(a, b, (((1,), (1,)), ((), ())), preferred_element_type=jnp.float32)


def round_f32(x):
    return x.astype(jnp.bfloat16).astype(jnp.float32)


def lanes_of(part):
    return slice(part * 128, part * 128 + 128)


def put_rows(dst, values, row, count):
    for part in range(BLK // 128):
        dst[part, row : row + count, 8:72, :] = values[:, lanes_of(part)].reshape(count, 64, 128)


def put_edge(dst, values, first, count, col):
    for part in range(BLK // 128):
        for r in range(count):
            dst[part, r, col : col + 1, :] = values[first + r : first + r + 1, lanes_of(part)]


def conv_row(src, part, row, taps):
    total = None
    for a in range(3):
        for b in range(3):
            term = src[part, row + a, 7 + b : 71 + b, :] * taps[a][b]
            total = term if total is None else total + term
    return total


def read_taps(dw, part, flip):
    taps = []
    for a in range(3):
        aa = 2 - a if flip else a
        order = (2, 1, 0) if flip else (0, 1, 2)
        taps.append([0.5 * dw[aa, b : b + 1, lanes_of(part)] for b in order])
    return taps


SLOTS = 8
BLOCK_ROWS = 40
SPAN = 64 * BLOCK_ROWS


def send_order(x, slot, parity):
    k = 8 * slot
    if k:
        x = jnp.concatenate([x[k:], x[:k]], axis=0)
    return pltpu.roll(x, (64 - 4 * parity) & 63, 0)


def receive_order(x, slot, parity):
    k = 8 * slot
    if k:
        x = jnp.concatenate([x[64 - k :], x[: 64 - k]], axis=0)
    return pltpu.roll(x, 4 * parity, 0)


def pack_for_owners(read, parity, packed_rows, out):
    for c in range(4):
        for row in range(16):
            x = send_order(read(row, lanes_of(c)), row % 8, parity)
            packed_rows[c, pl.ds(row // 8 * 512 + row % 8, 64, stride=SLOTS), :] = x
        out[:, lanes_of(c)] = packed_rows[c].astype(jnp.bfloat16)


def grad_att_kernel(place, grad, w_out, out, product, packed_rows):
    product[...] = nt(grad[...], w_out[...])
    pack_for_owners(
        lambda row, lanes: product[row * 64 : row * 64 + 64, lanes], place[0], packed_rows, out
    )


SMEM = pl.BlockSpec(memory_space=pltpu.SMEM)
VMEM = pl.BlockSpec(memory_space=pltpu.VMEM)


def grad_att_for_owners(place, grad, w_out):
    return pl.pallas_call(
        grad_att_kernel,
        out_shape=jax.ShapeDtypeStruct(grad.shape, jnp.bfloat16),
        in_specs=[SMEM, VMEM, VMEM],
        out_specs=VMEM,
        scratch_shapes=[
            pltpu.VMEM(grad.shape, jnp.float32),
            pltpu.VMEM((4, 1024, 128), jnp.float32),
        ],
        name="grad_att",
        compiler_params=pltpu.CompilerParams(vmem_limit_bytes=16 * 1024 * 1024),
    )(place, grad, w_out)


def finish_kernel(place, hidden, attn, out, rows_of):
    for c in range(4):
        rows_of[c] = attn[:, lanes_of(c)].astype(jnp.float32)
        for row in range(16):
            x = rows_of[c, pl.ds(row // 8 * 512 + row % 8, 64, stride=SLOTS), :]
            at = slice(row * 64, row * 64 + 64)
            total = hidden[at, lanes_of(c)].astype(jnp.float32) + receive_order(
                x, row % 8, place[0]
            )
            out[at, lanes_of(c)] = total.astype(jnp.bfloat16)


def finish(place, hidden, attn):
    return pl.pallas_call(
        finish_kernel,
        out_shape=jax.ShapeDtypeStruct(hidden.shape, jnp.bfloat16),
        in_specs=[SMEM, VMEM, VMEM],
        out_specs=VMEM,
        scratch_shapes=[pltpu.VMEM((4, 1024, 128), jnp.float32)],
        name="add_attention",
        compiler_params=pltpu.CompilerParams(vmem_limit_bytes=16 * 1024 * 1024),
    )(place, hidden, attn)


def fwd_kernel(place, top, mid, bot, left, right, w_exp, dw, w_proj, out, sent, act, acc, gout, packed_rows):
    step = pl.program_id(0)
    width = mid.shape[-1]
    w = w_exp[...] * jnp.bfloat16(0.5)

    @pl.when(step == 0)
    def _():
        acc[...] = mid[...].reshape(1024, width).astype(jnp.float32)

    def act_of(x):
        h = jnp.dot(x, w, preferred_element_type=jnp.float32)
        _, t = half_gelu(h)
        return round_f32(gelu_value(h, t))

    put_edge(act, act_of(left[...])[EDGE:], 1, 18, 7)
    put_edge(act, act_of(right[...])[:EDGE], 1, 18, 72)
    put_rows(act, act_of(top[1]), 0, 1)
    for r in range(0, 16, 4):
        put_rows(act, act_of(mid[r : r + 4].reshape(256, width)), 1 + r, 4)
    put_rows(act, act_of(bot[0]), 17, 1)

    for part in range(BLK // 128):
        taps = read_taps(dw, part, False)
        for r in range(16):
            h = conv_row(act, part, r, taps)
            _, t = half_gelu(h)
            gout[r * 64 : r * 64 + 64, lanes_of(part)] = gelu_value(h, t).astype(jnp.bfloat16)
    wp = w_proj[...]
    for r in range(0, 1024, 256):
        acc[r : r + 256] += jnp.dot(gout[r : r + 256], wp, preferred_element_type=jnp.float32)

    @pl.when(step == pl.num_programs(0) - 1)
    def _():
        out[...] = acc[...].astype(jnp.bfloat16)
        pack_for_owners(
            lambda row, lanes: acc[row * 64 : row * 64 + 64, lanes], place[0], packed_rows, sent
        )


def full(shape):
    return pl.BlockSpec(shape, lambda i: (0,) * len(shape))


def forward(place, top, mid, bot, left, right, w_exp, dw, w_proj):
    width, expand = w_exp.shape
    return pl.pallas_call(
        fwd_kernel,
        grid=(expand // BLK,),
        out_shape=(jax.ShapeDtypeStruct((1024, width), jnp.bfloat16),) * 2,
        in_specs=[
            SMEM, full(top.shape), full(mid.shape), full(bot.shape), full(left.shape),
            full(right.shape),
            pl.BlockSpec((width, BLK), lambda i: (0, i)),
            pl.BlockSpec((3, 3, BLK), lambda i: (0, 0, i)),
            pl.BlockSpec((BLK, width), lambda i: (i, 0)),
        ],
        out_specs=(full((1024, width)),) * 2,
        scratch_shapes=[
            pltpu.VMEM((BLK // 128, 18, FRAME, 128), jnp.float32),
            pltpu.VMEM((1024, width), jnp.float32),
            pltpu.VMEM((1024, BLK), jnp.bfloat16),
            pltpu.VMEM((4, 1024, 128), jnp.float32),
        ],
        name="mbconv_forward",
        compiler_params=pltpu.CompilerParams(vmem_limit_bytes=LIMIT),
    )(place, top, mid, bot, left, right, w_exp, dw, w_proj)


def slope_kernel(top, mid, bot, left, near_left, near_right, right, w_exp, dw,
                 pre_out, conv_out, edge_out, act, cols):
    width = mid.shape[-1]
    w = w_exp[...] * jnp.bfloat16(0.5)

    def act_of(x, slope_row=None):
        h = jnp.dot(x, w, preferred_element_type=jnp.float32)
        h2, t = half_gelu(h)
        if slope_row is not None:
            pre_out[slope_row * 64 : slope_row * 64 + x.shape[0], :] = double_slope(h, h2, t)
        return round_f32(gelu_value(h, t))

    for side, pair in enumerate((left, near_left, near_right, right)):
        a = act_of(pair[...])
        for part in range(BLK // 128):
            cols[part, 2 * side : 2 * side + 2, :, :] = a[:, lanes_of(part)].reshape(2, EDGE, 128)
        if side == 0:
            put_edge(act, a[EDGE:], 0, 20, 7)
        if side == 3:
            put_edge(act, a[:EDGE], 0, 20, 72)
    put_rows(act, act_of(top[...].reshape(128, width)), 0, 2)
    for r in range(0, 16, 4):
        put_rows(act, act_of(mid[r : r + 4].reshape(256, width), r), 2 + r, 4)
    put_rows(act, act_of(bot[...].reshape(128, width)), 18, 2)

    for part in range(BLK // 128):
        taps = read_taps(dw, part, False)
        for r in range(18):
            h = conv_row(act, part, r, taps)
            h2, t = half_gelu(h)
            conv_out[r * 64 : r * 64 + 64, lanes_of(part)] = double_slope(h, h2, t)
        for side in range(2):
            h = None
            for a in range(3):
                for b in range(3):
                    term = cols[part, 5 * side + b, a : a + 18, :] * taps[a][b]
                    h = term if h is None else h + term
            h2, t = half_gelu(h)
            edge_out[side * EDGE : side * EDGE + 18, lanes_of(part)] = double_slope(h, h2, t)
            edge_out[side * EDGE + 18 : side * EDGE + EDGE, lanes_of(part)] = jnp.zeros(
                (EDGE - 18, 128), jnp.float32
            )


def slopes(top, mid, bot, left, near_left, near_right, right, w_exp, dw, first, count):
    width = w_exp.shape[0]
    side = full(left.shape)
    rows = (1024, 18 * 64, 2 * EDGE)
    return pl.pallas_call(
        slope_kernel,
        grid=(count,),
        out_shape=tuple(jax.ShapeDtypeStruct((n, count * BLK), jnp.float32) for n in rows),
        in_specs=[
            full(top.shape), full(mid.shape), full(bot.shape), side, side, side, side,
            pl.BlockSpec((width, BLK), lambda i: (0, i + first)),
            pl.BlockSpec((3, 3, BLK), lambda i: (0, 0, i + first)),
        ],
        out_specs=tuple(pl.BlockSpec((n, BLK), lambda i: (0, i)) for n in rows),
        scratch_shapes=[
            pltpu.VMEM((BLK // 128, 20, FRAME, 128), jnp.float32),
            pltpu.VMEM((BLK // 128, 8, EDGE, 128), jnp.float32),
        ],
        name="mbconv_slopes",
        compiler_params=pltpu.CompilerParams(vmem_limit_bytes=LIMIT),
    )(top, mid, bot, left, near_left, near_right, right, w_exp, dw)


def bwd_kernel(split, place, top, grad, back, bot, left, right, *rest):
    tables, rest = rest[:6], rest[6:]
    w_exp, dw, w_proj, out, mixed, pre, acc, rounded, got, ends, sides = rest
    step = pl.program_id(0)

    @pl.when(step == 0)
    def _():
        parity = place[0]
        got[...] = back[...].astype(jnp.float32)

        def tokens_of(half, slot, c):
            return got[pl.ds(half * SPAN + c * 10 + slot, 64, stride=BLOCK_ROWS), :]

        def token_of(half, shift, column, c):
            owner = (column + 128 - shift) & 63
            return got[pl.ds(half * SPAN + owner * BLOCK_ROWS + c * 10 + 9, 1), :]

        for c in range(4):
            lanes = lanes_of(c)
            for row in range(16):
                at = slice(row * 64, row * 64 + 64)
                x = receive_order(tokens_of(row // 8, row % 8, c), row % 8, parity)
                total = grad[at, lanes].astype(jnp.float32) + x
                acc[at, lanes] = total
                rounded[at, lanes] = total.astype(jnp.bfloat16)
            low = receive_order(tokens_of(0, 8, c), 0, 1 - parity)
            ends[64:128, lanes] = (bot[:, lanes].astype(jnp.float32) + low).astype(jnp.bfloat16)
            high = receive_order(tokens_of(1, 8, c), 7, 1 - parity)
            ends[0:64, lanes] = (top[:, lanes].astype(jnp.float32) + high).astype(jnp.bfloat16)
            for side, (halo, column) in enumerate(((left, 63), (right, 0))):
                sides[side, :, lanes] = halo[:, lanes].astype(jnp.float32)
                for i in range(18):
                    half, slot, flip = (i - 1) // 8, (i - 1) % 8, parity
                    if i == 0:
                        half, slot, flip = 1, 7, 1 - parity
                    if i == 17:
                        half, slot, flip = 0, 0, 1 - parity
                    sides[side, i : i + 1, lanes] += token_of(
                        half, 8 * slot + 4 * flip, column, c
                    )

    def work(pre_slope, conv_slope, edge_slope):
        wp = w_proj[...] * jnp.bfloat16(0.5)
        for side, col in enumerate((7, 72)):
            edge = nt(sides[side].astype(jnp.bfloat16), wp)
            edge = edge * edge_slope[side * EDGE : side * EDGE + EDGE]
            put_edge(mixed, round_f32(edge), 0, 18, col)

        def put(x, row, count):
            mid = nt(x, wp) * conv_slope[row * 64 : (row + count) * 64]
            put_rows(mixed, round_f32(mid), row, count)

        put(ends[0:64], 0, 1)
        for r in range(0, 16, 4):
            put(rounded[r * 64 : r * 64 + 256], 1 + r, 4)
        put(ends[64:128], 17, 1)

        for part in range(BLK // 128):
            taps = read_taps(dw, part, True)
            for r in range(16):
                rows = slice(r * 64, r * 64 + 64)
                z = conv_row(mixed, part, r, taps) * pre_slope[rows, lanes_of(part)]
                pre[rows, lanes_of(part)] = z.astype(jnp.bfloat16)
        w = w_exp[...]
        for r in range(0, 1024, 256):
            acc[r : r + 256] += nt(pre[r : r + 256], w)

    @pl.when(step < split)
    def _():
        work(*tables[:3])

    @pl.when(step >= split)
    def _():
        work(*tables[3:])

    @pl.when(step == pl.num_programs(0) - 1)
    def _():
        out[...] = acc[...].astype(jnp.bfloat16)


def backward(place, top, grad, back, bot, left, right, early, late, w_exp, dw, w_proj):
    width, expand = w_exp.shape
    split = early[0].shape[1] // BLK
    return pl.pallas_call(
        functools.partial(bwd_kernel, split),
        grid=(expand // BLK,),
        out_shape=jax.ShapeDtypeStruct((1024, width), jnp.bfloat16),
        in_specs=[
            SMEM, full(top.shape), full(grad.shape), full(back.shape), full(bot.shape),
            full(left.shape), full(right.shape),
            *(pl.BlockSpec((x.shape[0], BLK), lambda i: (0, jnp.minimum(i, split - 1)))
              for x in early),
            *(pl.BlockSpec((x.shape[0], BLK), lambda i: (0, jnp.maximum(i - split, 0)))
              for x in late),
            pl.BlockSpec((width, BLK), lambda i: (0, i)),
            pl.BlockSpec((3, 3, BLK), lambda i: (0, 0, i)),
            pl.BlockSpec((BLK, width), lambda i: (i, 0)),
        ],
        out_specs=full((1024, width)),
        scratch_shapes=[
            pltpu.VMEM((BLK // 128, 18, FRAME, 128), jnp.float32),
            pltpu.VMEM((1024, BLK), jnp.bfloat16),
            pltpu.VMEM((1024, width), jnp.float32),
            pltpu.VMEM((1024, width), jnp.bfloat16),
            pltpu.VMEM(back.shape, jnp.float32),
            pltpu.VMEM((128, width), jnp.bfloat16),
            pltpu.VMEM((2, EDGE, width), jnp.float32),
        ],
        name="mbconv_backward",
        compiler_params=pltpu.CompilerParams(vmem_limit_bytes=LIMIT),
    )(place, top, grad, back, bot, left, right, *early, *late, w_exp, dw, w_proj)


WINDOWS = 16
GROUP = 4
BREADTH = 2


def gather_window(src, start):
    return jnp.concatenate(
        [src[c, pl.ds(start, 64, stride=SLOTS), :] for c in range(4)], axis=1
    )


def scatter_window(dst, start, values):
    for c in range(4):
        dst[c, pl.ds(start, 64, stride=SLOTS), :] = values[:, lanes_of(c)]


def return_slots(place, dst):
    half, owner = place[0], place[1]
    member = lax.broadcasted_iota(jnp.int32, (64, 128), 0)
    for parity in range(2):
        other = 1 - parity
        edge_slot = 7 * half
        row_shift = 1 - half if parity == 1 else -half
        near = owner + 4 * parity
        at_left = (near & 7) == 0
        at_right = (near & 7) == 7
        column = (owner + 8 * edge_slot + 4 * other) & 63
        corner_left = column == 0
        corner_right = column == 63
        side = at_left | at_right
        line = jnp.where(at_left, (64 - near) >> 3, (127 - near) >> 3) & 7
        start = jnp.where(side, parity * SPAN + line, other * SPAN + edge_slot)
        rows_on = jnp.where(side, 0, row_shift)
        cols_on = jnp.where(at_left | corner_left, 1, -1)
        exists = side | corner_left | corner_right
        cases = (
            (8, other * SPAN + edge_slot, row_shift, 0, half >= 0),
            (9, start, rows_on, cols_on, exists),
        )
        for slot, begin, dq, dc, there in cases:
            q = (member >> 3) + dq
            c = (member & 7) + dc
            limit = jnp.where(there, 8, 0)
            valid = (q >= 0) & (q < limit) & (c >= 0) & (c < 8)
            shift = (64 - 8 * dq - dc) & 63
            for chunk in range(4):
                x = dst[pl.ds(begin + chunk * 10, 64, stride=BLOCK_ROWS), :]
                x = jnp.where(valid, pltpu.roll(x, shift, 0), 0.0)
                dst[pl.ds(parity * SPAN + chunk * 10 + slot, 64, stride=BLOCK_ROWS), :] = x


def attend_kernel(place, hid, gatt, gain, w_qkv, back_out, att_out, hs, gs, sends, packed, gpack):
    scale = 32 ** (-0.5)
    for c in range(4):
        hs[c] = hid[:, c * 128 : c * 128 + 128].astype(jnp.float32)
        gs[c] = gatt[:, c * 128 : c * 128 + 128].astype(jnp.float32)
    lane = lax.broadcasted_iota(jnp.int32, (64, 128), 1)
    masks = [(lane >= 32 * h) & (lane < 32 * h + 32) for h in range(4)]
    gain_row = gain[...]

    def spread(x):
        zero = jnp.zeros_like(x)
        return jnp.concatenate([jnp.where(m, x, zero) for m in masks], axis=0)

    def collect(y):
        total = None
        for h in range(4):
            term = jnp.where(masks[h], y[h * 64 : h * 64 + 64], 0.0)
            total = term if total is None else total + term
        return total

    def tn(a, b):
        return lax.dot_general(a, b, (((0,), (0,)), ((), ())), preferred_element_type=jnp.float32)

    def body(group, carry):
        parity, slot = group // 2, (group % 2) * GROUP
        base = parity * 512 + slot
        sent = parity * SPAN + slot
        x = jnp.concatenate([gather_window(hs, base + i) for i in range(GROUP)], axis=0)
        center = x - jnp.mean(x, axis=-1, keepdims=True)
        inv_std = lax.rsqrt(jnp.mean(center * center, axis=-1, keepdims=True) + 1e-5)
        unit = center * inv_std
        normed = (unit * gain_row).astype(jnp.bfloat16)
        packed[...] = jnp.dot(normed, w_qkv[...], preferred_element_type=jnp.float32).astype(
            jnp.bfloat16
        )
        units = [(i, hg) for i in range(GROUP) for hg in range(4)]
        g_all = [gather_window(gs, base + i).astype(jnp.bfloat16) for i in range(GROUP)]
        outs = {}
        for first in range(0, len(units), BREADTH):
            batch = units[first : first + BREADTH]
            st = []
            for i, hg in batch:
                rows = slice(i * 64, i * 64 + 64)
                lo = hg * 128
                k = packed[rows, 512 + lo : 512 + lo + 128]
                v = packed[rows, 1024 + lo : 1024 + lo + 128]
                q_bd = spread(packed[rows, lo : lo + 128])
                g_bd = spread(g_all[i][:, lo : lo + 128])
                st.append((k, v, q_bd, g_bd))
            sd = [(nt(k, q_bd), nt(v, g_bd)) for k, v, q_bd, g_bd in st]
            soft = []
            for s, dp in sd:
                s = s * scale
                e = jnp.exp(s - jnp.max(s, axis=0, keepdims=True))
                p = e * (1.0 / jnp.sum(e, axis=0, keepdims=True))
                dot = jnp.sum(dp * p, axis=0, keepdims=True)
                soft.append((p.astype(jnp.bfloat16), (p * (dp - dot) * scale).astype(jnp.bfloat16)))
            prods = []
            for (k, v, q_bd, g_bd), (p, ds) in zip(st, soft):
                prods.append((
                    jnp.dot(p, g_bd, preferred_element_type=jnp.float32),
                    jnp.dot(ds, q_bd, preferred_element_type=jnp.float32),
                    tn(ds, k),
                    tn(p, v),
                ))
            for (i, hg), (dv, dk, dq, o) in zip(batch, prods):
                rows = slice(i * 64, i * 64 + 64)
                lo = hg * 128
                gpack[rows, lo : lo + 128] = collect(dq).astype(jnp.bfloat16)
                gpack[rows, 512 + lo : 512 + lo + 128] = dk.astype(jnp.bfloat16)
                gpack[rows, 1024 + lo : 1024 + lo + 128] = dv.astype(jnp.bfloat16)
                outs[i, hg] = collect(o)
        for i in range(GROUP):
            scatter_window(gs, base + i, jnp.concatenate([outs[i, hg] for hg in range(4)], axis=1))
        scaled = nt(gpack[...], w_qkv[...]) * gain_row
        grad = inv_std * (
            scaled
            - jnp.mean(scaled, axis=-1, keepdims=True)
            - unit * jnp.mean(scaled * unit, axis=-1, keepdims=True)
        )
        for i in range(GROUP):
            for c in range(4):
                sends[pl.ds(sent + i + c * 10, 64, stride=BLOCK_ROWS), :] = grad[
                    i * 64 : i * 64 + 64, lanes_of(c)
                ]
        return carry

    lax.fori_loop(0, WINDOWS // GROUP, body, 0)
    return_slots(place, sends)
    back_out[...] = sends[...].astype(jnp.bfloat16)
    for c in range(4):
        att_out[:, c * 128 : c * 128 + 128] = gs[c].astype(jnp.bfloat16)


def attend(place, hid, gatt, gain, w_qkv):
    blocks = (128 * BLOCK_ROWS, 128)
    return pl.pallas_call(
        attend_kernel,
        out_shape=(
            jax.ShapeDtypeStruct(blocks, jnp.bfloat16),
            jax.ShapeDtypeStruct(hid.shape, jnp.bfloat16),
        ),
        in_specs=[SMEM] + [VMEM] * 4,
        out_specs=(VMEM, VMEM),
        scratch_shapes=[
            pltpu.VMEM((4, 1024, 128), jnp.float32),
            pltpu.VMEM((4, 1024, 128), jnp.float32),
            pltpu.VMEM(blocks, jnp.float32),
            pltpu.VMEM((GROUP * 64, 1536), jnp.bfloat16),
            pltpu.VMEM((GROUP * 64, 1536), jnp.bfloat16),
        ],
        name="window_attention",
        compiler_params=pltpu.CompilerParams(vmem_limit_bytes=48 * 1024 * 1024),
    )(place, hid, gatt, gain, w_qkv)


def neighbour_pair(axis, size, to_next, to_prev):
    up = [(i, i + 1) for i in range(size - 1)]
    down = [(i + 1, i) for i in range(size - 1)]
    return lax.ppermute(to_next, axis, up), lax.ppermute(to_prev, axis, down)


def edge_columns(parts):
    rows = jnp.concatenate(parts, axis=0).transpose(1, 0, 2)
    rows = jnp.pad(rows, ((0, 0), (0, EDGE - rows.shape[1]), (0, 0)))
    return rows.reshape(-1, rows.shape[2])


EARLY = 5


def per_device(tokens, grad_output, w_exp, dw_kernel, w_proj, ln_gain, w_qkv, w_out):
    rows, cols, width = tokens.shape
    blocks = w_exp.shape[1] // BLK
    row_count = lax.axis_size("row")
    col_count = lax.axis_size("col")
    groups = [
        [
            (2 * q + h) * col_count + c
            for h in range(2)
            for q in range(row_count // 2)
            for c in range(col_count)
        ]
    ]
    row_at, col_at = lax.axis_index("row"), lax.axis_index("col")
    place = jnp.stack([row_at % 2, row_at // 2 * col_count + col_at]).astype(jnp.int32)

    def exchange(flat):
        sent = flat.reshape(row_count * col_count, -1, flat.shape[1])
        moved = lax.all_to_all(
            sent, ("row", "col"), split_axis=0, concat_axis=0, tiled=True,
            axis_index_groups=groups,
        )
        return moved.reshape(flat.shape)

    from_top, from_bot = neighbour_pair(
        "row",
        row_count,
        jnp.concatenate([tokens[rows - 2 :], grad_output[rows - 1 :]], axis=0),
        jnp.concatenate([tokens[:2], grad_output[:1]], axis=0),
    )
    top, g_top, bot, g_bot = from_top[:2], from_top[2:], from_bot[:2], from_bot[2:]
    grad_flat = grad_output.reshape(rows * cols, width)
    grad_win = exchange(grad_att_for_owners(place, grad_flat, w_out))

    near_right = edge_columns([x[:, cols - 2 :] for x in (top, tokens, bot)])
    near_left = edge_columns([x[:, :2] for x in (top, tokens, bot)])
    grad_right = edge_columns([x[:, cols - 1 :] for x in (g_top, grad_output, g_bot)])
    grad_left = edge_columns([x[:, :1] for x in (g_top, grad_output, g_bot)])
    from_left, from_right = neighbour_pair(
        "col",
        col_count,
        jnp.concatenate([near_right, grad_right], axis=0),
        jnp.concatenate([near_left, grad_left], axis=0),
    )
    left, g_left = from_left[: 2 * EDGE], from_left[2 * EDGE :]
    right, g_right = from_right[: 2 * EDGE], from_right[2 * EDGE :]

    hidden, sent = forward(place, top, tokens, bot, left, right, w_exp, dw_kernel, w_proj)
    sent, grad_win = lax.optimization_barrier((sent, grad_win))
    hidden_win = exchange(sent)
    w_late, _ = lax.optimization_barrier((w_exp, sent))
    halo = (top, tokens, bot, left, near_left, near_right, right)
    early = slopes(*halo, w_late, dw_kernel, 0, EARLY)
    hidden_win, *early = lax.optimization_barrier((hidden_win, *early))
    back_win, att_win = attend(place, hidden_win, grad_win, ln_gain.reshape(1, width), w_qkv)
    back = exchange(back_win)
    w_last, att_win = lax.optimization_barrier((w_exp, att_win))
    late = slopes(*halo, w_last, dw_kernel, EARLY, blocks - EARLY)
    attn_win = jnp.dot(att_win, w_out, preferred_element_type=jnp.float32).astype(jnp.bfloat16)
    back, attn_win, *late = lax.optimization_barrier((back, attn_win, *late))
    attn = exchange(attn_win)
    grad_tokens = backward(
        place, g_top.reshape(cols, width), grad_flat, back, g_bot.reshape(cols, width),
        g_left, g_right, early, late, w_exp, dw_kernel, w_proj,
    )
    attn, grad_tokens = lax.optimization_barrier((attn, grad_tokens))
    output = finish(place, hidden, attn)
    return output.reshape(tokens.shape), grad_tokens.reshape(tokens.shape)


def solution(mesh):
    in_specs = (P("row", "col", None), P("row", "col", None), P(), P(), P(), P(), P(), P())
    out_specs = (P("row", "col", None), P("row", "col", None))
    return jax.shard_map(
        per_device, mesh=mesh, in_specs=in_specs, out_specs=out_specs, check_vma=False
    )
```

```python
import jax
import jax.numpy as jnp
from jax import lax
from jax.experimental import pallas as pl
from jax.experimental.pallas import tpu as pltpu
from jax.sharding import PartitionSpec as P


C0 = 0.7978845608028654
C1 = C0 * 0.044715
BLK = 256
FRAME = 80
EDGE = 24
LIMIT = 60 * 1024 * 1024


def half_gelu(h):
    h2 = h * h
    return h2, jnp.tanh(h * ((2.0 * C0) + (8.0 * C1) * h2))


def gelu_value(h, t):
    return h + h * t


def double_slope(h, h2, t):
    return (1.0 + t) + (1.0 - t * t) * (h * ((2.0 * C0) + (24.0 * C1) * h2))


def nt(a, b):
    return lax.dot_general(a, b, (((1,), (1,)), ((), ())), preferred_element_type=jnp.float32)


def round_f32(x):
    return x.astype(jnp.bfloat16).astype(jnp.float32)


def lanes_of(part):
    return slice(part * 128, part * 128 + 128)


def put_rows(dst, values, row, count):
    for part in range(BLK // 128):
        dst[part, row : row + count, 8:72, :] = values[:, lanes_of(part)].reshape(count, 64, 128)


def put_edge(dst, values, first, count, col):
    for part in range(BLK // 128):
        for r in range(count):
            dst[part, r, col : col + 1, :] = values[first + r : first + r + 1, lanes_of(part)]


def conv_row(src, part, row, taps):
    total = None
    for a in range(3):
        for b in range(3):
            term = src[part, row + a, 7 + b : 71 + b, :] * taps[a][b]
            total = term if total is None else total + term
    return total


def read_taps(dw, part, flip):
    taps = []
    for a in range(3):
        aa = 2 - a if flip else a
        order = (2, 1, 0) if flip else (0, 1, 2)
        taps.append([0.5 * dw[aa, b : b + 1, lanes_of(part)] for b in order])
    return taps


SLOTS = 8
BLOCK_ROWS = 40
SPAN = 64 * BLOCK_ROWS


def send_order(x, slot, parity):
    k = 8 * slot
    if k:
        x = jnp.concatenate([x[k:], x[:k]], axis=0)
    return pltpu.roll(x, (64 - 4 * parity) & 63, 0)


def receive_order(x, slot, parity):
    k = 8 * slot
    if k:
        x = jnp.concatenate([x[64 - k :], x[: 64 - k]], axis=0)
    return pltpu.roll(x, 4 * parity, 0)


def pack_for_owners(read, parity, packed_rows, out):
    for c in range(4):
        for row in range(16):
            x = send_order(read(row, lanes_of(c)), row % 8, parity)
            packed_rows[c, pl.ds(row // 8 * 512 + row % 8, 64, stride=SLOTS), :] = x
        out[:, lanes_of(c)] = packed_rows[c].astype(jnp.bfloat16)


def grad_att_kernel(place, grad, w_out, out, product, packed_rows):
    product[...] = nt(grad[...], w_out[...])
    pack_for_owners(
        lambda row, lanes: product[row * 64 : row * 64 + 64, lanes], place[0], packed_rows, out
    )


SMEM = pl.BlockSpec(memory_space=pltpu.SMEM)
VMEM = pl.BlockSpec(memory_space=pltpu.VMEM)


def grad_att_for_owners(place, grad, w_out):
    return pl.pallas_call(
        grad_att_kernel,
        out_shape=jax.ShapeDtypeStruct(grad.shape, jnp.bfloat16),
        in_specs=[SMEM, VMEM, VMEM],
        out_specs=VMEM,
        scratch_shapes=[
            pltpu.VMEM(grad.shape, jnp.float32),
            pltpu.VMEM((4, 1024, 128), jnp.float32),
        ],
        name="grad_att",
        compiler_params=pltpu.CompilerParams(vmem_limit_bytes=16 * 1024 * 1024),
    )(place, grad, w_out)


def finish_kernel(place, hidden, attn, out, rows_of):
    for c in range(4):
        rows_of[c] = attn[:, lanes_of(c)].astype(jnp.float32)
        for row in range(16):
            x = rows_of[c, pl.ds(row // 8 * 512 + row % 8, 64, stride=SLOTS), :]
            at = slice(row * 64, row * 64 + 64)
            total = hidden[at, lanes_of(c)].astype(jnp.float32) + receive_order(
                x, row % 8, place[0]
            )
            out[at, lanes_of(c)] = total.astype(jnp.bfloat16)


def finish(place, hidden, attn):
    return pl.pallas_call(
        finish_kernel,
        out_shape=jax.ShapeDtypeStruct(hidden.shape, jnp.bfloat16),
        in_specs=[SMEM, VMEM, VMEM],
        out_specs=VMEM,
        scratch_shapes=[pltpu.VMEM((4, 1024, 128), jnp.float32)],
        name="add_attention",
        compiler_params=pltpu.CompilerParams(vmem_limit_bytes=16 * 1024 * 1024),
    )(place, hidden, attn)


def fwd_kernel(place, top, mid, bot, left, right, w_exp, dw, w_proj, out, sent, act, acc, gout, packed_rows):
    step = pl.program_id(0)
    width = mid.shape[-1]
    w = w_exp[...] * jnp.bfloat16(0.5)

    @pl.when(step == 0)
    def _():
        acc[...] = mid[...].reshape(1024, width).astype(jnp.float32)

    def act_of(x):
        h = jnp.dot(x, w, preferred_element_type=jnp.float32)
        _, t = half_gelu(h)
        return round_f32(gelu_value(h, t))

    put_edge(act, act_of(left[: 2 * EDGE])[EDGE:], 1, 18, 7)
    put_edge(act, act_of(right[: 2 * EDGE])[:EDGE], 1, 18, 72)
    put_rows(act, act_of(top[1]), 0, 1)
    for r in range(0, 16, 4):
        put_rows(act, act_of(mid[r : r + 4].reshape(256, width)), 1 + r, 4)
    put_rows(act, act_of(bot[0]), 17, 1)

    for part in range(BLK // 128):
        taps = read_taps(dw, part, False)
        for r in range(16):
            h = conv_row(act, part, r, taps)
            _, t = half_gelu(h)
            gout[r * 64 : r * 64 + 64, lanes_of(part)] = gelu_value(h, t).astype(jnp.bfloat16)
    wp = w_proj[...]
    for r in range(0, 1024, 256):
        acc[r : r + 256] += jnp.dot(gout[r : r + 256], wp, preferred_element_type=jnp.float32)

    @pl.when(step == pl.num_programs(0) - 1)
    def _():
        out[...] = acc[...].astype(jnp.bfloat16)
        pack_for_owners(
            lambda row, lanes: acc[row * 64 : row * 64 + 64, lanes], place[0], packed_rows, sent
        )


def full(shape):
    return pl.BlockSpec(shape, lambda i: (0,) * len(shape))


def forward(place, top, mid, bot, left, right, w_exp, dw, w_proj):
    width, expand = w_exp.shape
    return pl.pallas_call(
        fwd_kernel,
        grid=(expand // BLK,),
        out_shape=(jax.ShapeDtypeStruct((1024, width), jnp.bfloat16),) * 2,
        in_specs=[
            SMEM, full(top.shape), full(mid.shape), full(bot.shape), full(left.shape),
            full(right.shape),
            pl.BlockSpec((width, BLK), lambda i: (0, i)),
            pl.BlockSpec((3, 3, BLK), lambda i: (0, 0, i)),
            pl.BlockSpec((BLK, width), lambda i: (i, 0)),
        ],
        out_specs=(full((1024, width)),) * 2,
        scratch_shapes=[
            pltpu.VMEM((BLK // 128, 18, FRAME, 128), jnp.float32),
            pltpu.VMEM((1024, width), jnp.float32),
            pltpu.VMEM((1024, BLK), jnp.bfloat16),
            pltpu.VMEM((4, 1024, 128), jnp.float32),
        ],
        name="mbconv_forward",
        compiler_params=pltpu.CompilerParams(vmem_limit_bytes=LIMIT),
    )(place, top, mid, bot, left, right, w_exp, dw, w_proj)


def slope_kernel(top, mid, bot, left, near_left, near_right, right, w_exp, dw, *rest):
    pre_out, conv_out, edge_out, act, cols = rest[-5:]
    width = mid.shape[-1]
    w = w_exp[...] * jnp.bfloat16(0.5)

    def act_of(x, slope_row=None):
        h = jnp.dot(x, w, preferred_element_type=jnp.float32)
        h2, t = half_gelu(h)
        if slope_row is not None:
            pre_out[slope_row * 64 : slope_row * 64 + x.shape[0], :] = double_slope(h, h2, t)
        return round_f32(gelu_value(h, t))

    for side, pair in enumerate((left, near_left, near_right, right)):
        a = act_of(pair[: 2 * EDGE])
        for part in range(BLK // 128):
            cols[part, 2 * side : 2 * side + 2, :, :] = a[:, lanes_of(part)].reshape(2, EDGE, 128)
        if side == 0:
            put_edge(act, a[EDGE:], 0, 20, 7)
        if side == 3:
            put_edge(act, a[:EDGE], 0, 20, 72)
    put_rows(act, act_of(top[:2].reshape(128, width)), 0, 2)
    for r in range(0, 16, 4):
        put_rows(act, act_of(mid[r : r + 4].reshape(256, width), r), 2 + r, 4)
    put_rows(act, act_of(bot[:2].reshape(128, width)), 18, 2)

    for part in range(BLK // 128):
        taps = read_taps(dw, part, False)
        for r in range(18):
            h = conv_row(act, part, r, taps)
            h2, t = half_gelu(h)
            conv_out[r * 64 : r * 64 + 64, lanes_of(part)] = double_slope(h, h2, t)
        for side in range(2):
            h = None
            for a in range(3):
                for b in range(3):
                    term = cols[part, 5 * side + b, a : a + 18, :] * taps[a][b]
                    h = term if h is None else h + term
            h2, t = half_gelu(h)
            edge_out[side * EDGE : side * EDGE + 18, lanes_of(part)] = double_slope(h, h2, t)
            edge_out[side * EDGE + 18 : side * EDGE + EDGE, lanes_of(part)] = jnp.zeros(
                (EDGE - 18, 128), jnp.float32
            )


def slopes(top, mid, bot, left, near_left, near_right, right, w_exp, dw, first, count, done=()):
    width, expand = w_exp.shape
    rows = (1024, 18 * 64, 2 * EDGE)
    operands = (top, mid, bot, left, near_left, near_right, right)
    return pl.pallas_call(
        slope_kernel,
        grid=(count,),
        out_shape=tuple(jax.ShapeDtypeStruct((n, expand), jnp.float32) for n in rows),
        in_specs=[
            *(full(x.shape) for x in operands),
            pl.BlockSpec((width, BLK), lambda i: (0, i + first)),
            pl.BlockSpec((3, 3, BLK), lambda i: (0, 0, i + first)),
            *(pl.BlockSpec(memory_space=pl.ANY) for _ in done),
        ],
        out_specs=tuple(pl.BlockSpec((n, BLK), lambda i: (0, i + first)) for n in rows),
        input_output_aliases={9 + i: i for i in range(len(done))},
        scratch_shapes=[
            pltpu.VMEM((BLK // 128, 20, FRAME, 128), jnp.float32),
            pltpu.VMEM((BLK // 128, 8, EDGE, 128), jnp.float32),
        ],
        name="mbconv_slopes",
        compiler_params=pltpu.CompilerParams(vmem_limit_bytes=LIMIT),
    )(*operands, w_exp, dw, *done)


def bwd_kernel(place, top, grad, back, bot, left, right, pre_slope, conv_slope, edge_slope,
               w_exp, dw, w_proj, out, mixed, pre, acc, rounded, got, ends, sides):
    step = pl.program_id(0)

    @pl.when(step == 0)
    def _():
        parity = place[0]
        got[...] = back[...].astype(jnp.float32)

        def tokens_of(half, slot, c):
            return got[pl.ds(half * SPAN + c * 10 + slot, 64, stride=BLOCK_ROWS), :]

        def token_of(half, shift, column, c):
            owner = (column + 128 - shift) & 63
            return got[pl.ds(half * SPAN + owner * BLOCK_ROWS + c * 10 + 9, 1), :]

        for c in range(4):
            lanes = lanes_of(c)
            for row in range(16):
                at = slice(row * 64, row * 64 + 64)
                x = receive_order(tokens_of(row // 8, row % 8, c), row % 8, parity)
                total = grad[at, lanes].astype(jnp.float32) + x
                acc[at, lanes] = total
                rounded[at, lanes] = total.astype(jnp.bfloat16)
            low = receive_order(tokens_of(0, 8, c), 0, 1 - parity)
            ends[64:128, lanes] = (bot[2, :, lanes].astype(jnp.float32) + low).astype(jnp.bfloat16)
            high = receive_order(tokens_of(1, 8, c), 7, 1 - parity)
            ends[0:64, lanes] = (top[2, :, lanes].astype(jnp.float32) + high).astype(jnp.bfloat16)
            for side, (halo, column) in enumerate(((left, 63), (right, 0))):
                sides[side, :, lanes] = halo[:, lanes].astype(jnp.float32)[2 * EDGE :]
                for i in range(18):
                    half, slot, flip = (i - 1) // 8, (i - 1) % 8, parity
                    if i == 0:
                        half, slot, flip = 1, 7, 1 - parity
                    if i == 17:
                        half, slot, flip = 0, 0, 1 - parity
                    sides[side, i : i + 1, lanes] += token_of(
                        half, 8 * slot + 4 * flip, column, c
                    )

    wp = w_proj[...] * jnp.bfloat16(0.5)
    for side, col in enumerate((7, 72)):
        edge = nt(sides[side].astype(jnp.bfloat16), wp)
        edge = edge * edge_slope[side * EDGE : side * EDGE + EDGE]
        put_edge(mixed, round_f32(edge), 0, 18, col)

    def put(x, row, count):
        mid = nt(x, wp) * conv_slope[row * 64 : (row + count) * 64]
        put_rows(mixed, round_f32(mid), row, count)

    put(ends[0:64], 0, 1)
    for r in range(0, 16, 4):
        put(rounded[r * 64 : r * 64 + 256], 1 + r, 4)
    put(ends[64:128], 17, 1)

    for part in range(BLK // 128):
        taps = read_taps(dw, part, True)
        for r in range(16):
            rows = slice(r * 64, r * 64 + 64)
            z = conv_row(mixed, part, r, taps) * pre_slope[rows, lanes_of(part)]
            pre[rows, lanes_of(part)] = z.astype(jnp.bfloat16)
    w = w_exp[...]
    for r in range(0, 1024, 256):
        acc[r : r + 256] += nt(pre[r : r + 256], w)

    @pl.when(step == pl.num_programs(0) - 1)
    def _():
        out[...] = acc[...].astype(jnp.bfloat16)


def backward(place, top, grad, back, bot, left, right, tables, w_exp, dw, w_proj):
    width, expand = w_exp.shape
    return pl.pallas_call(
        bwd_kernel,
        grid=(expand // BLK,),
        out_shape=jax.ShapeDtypeStruct((1024, width), jnp.bfloat16),
        in_specs=[
            SMEM, full(top.shape), full(grad.shape), full(back.shape), full(bot.shape),
            full(left.shape), full(right.shape),
            *(pl.BlockSpec((x.shape[0], BLK), lambda i: (0, i)) for x in tables),
            pl.BlockSpec((width, BLK), lambda i: (0, i)),
            pl.BlockSpec((3, 3, BLK), lambda i: (0, 0, i)),
            pl.BlockSpec((BLK, width), lambda i: (i, 0)),
        ],
        out_specs=full((1024, width)),
        scratch_shapes=[
            pltpu.VMEM((BLK // 128, 18, FRAME, 128), jnp.float32),
            pltpu.VMEM((1024, BLK), jnp.bfloat16),
            pltpu.VMEM((1024, width), jnp.float32),
            pltpu.VMEM((1024, width), jnp.bfloat16),
            pltpu.VMEM(back.shape, jnp.float32),
            pltpu.VMEM((128, width), jnp.bfloat16),
            pltpu.VMEM((2, EDGE, width), jnp.float32),
        ],
        name="mbconv_backward",
        compiler_params=pltpu.CompilerParams(vmem_limit_bytes=LIMIT),
    )(place, top, grad, back, bot, left, right, *tables, w_exp, dw, w_proj)


WINDOWS = 16
GROUP = 4
BREADTH = 2


def gather_window(src, start):
    return jnp.concatenate(
        [src[c, pl.ds(start, 64, stride=SLOTS), :] for c in range(4)], axis=1
    )


def scatter_window(dst, start, values):
    for c in range(4):
        dst[c, pl.ds(start, 64, stride=SLOTS), :] = values[:, lanes_of(c)]


def return_slots(place, dst):
    half, owner = place[0], place[1]
    member = lax.broadcasted_iota(jnp.int32, (64, 128), 0)
    for parity in range(2):
        other = 1 - parity
        edge_slot = 7 * half
        row_shift = 1 - half if parity == 1 else -half
        near = owner + 4 * parity
        at_left = (near & 7) == 0
        at_right = (near & 7) == 7
        column = (owner + 8 * edge_slot + 4 * other) & 63
        corner_left = column == 0
        corner_right = column == 63
        side = at_left | at_right
        line = jnp.where(at_left, (64 - near) >> 3, (127 - near) >> 3) & 7
        start = jnp.where(side, parity * SPAN + line, other * SPAN + edge_slot)
        rows_on = jnp.where(side, 0, row_shift)
        cols_on = jnp.where(at_left | corner_left, 1, -1)
        exists = side | corner_left | corner_right
        cases = (
            (8, other * SPAN + edge_slot, row_shift, 0, half >= 0),
            (9, start, rows_on, cols_on, exists),
        )
        for slot, begin, dq, dc, there in cases:
            q = (member >> 3) + dq
            c = (member & 7) + dc
            limit = jnp.where(there, 8, 0)
            valid = (q >= 0) & (q < limit) & (c >= 0) & (c < 8)
            shift = (64 - 8 * dq - dc) & 63
            for chunk in range(4):
                x = dst[pl.ds(begin + chunk * 10, 64, stride=BLOCK_ROWS), :]
                x = jnp.where(valid, pltpu.roll(x, shift, 0), 0.0)
                dst[pl.ds(parity * SPAN + chunk * 10 + slot, 64, stride=BLOCK_ROWS), :] = x


def attend_kernel(place, hid, gatt, gain, w_qkv, back_out, att_out, hs, gs, sends, packed, gpack):
    scale = 32 ** (-0.5)
    for c in range(4):
        hs[c] = hid[:, c * 128 : c * 128 + 128].astype(jnp.float32)
        gs[c] = gatt[:, c * 128 : c * 128 + 128].astype(jnp.float32)
    lane = lax.broadcasted_iota(jnp.int32, (64, 128), 1)
    masks = [(lane >= 32 * h) & (lane < 32 * h + 32) for h in range(4)]
    gain_row = gain[...]

    def spread(x):
        zero = jnp.zeros_like(x)
        return jnp.concatenate([jnp.where(m, x, zero) for m in masks], axis=0)

    def collect(y):
        total = None
        for h in range(4):
            term = jnp.where(masks[h], y[h * 64 : h * 64 + 64], 0.0)
            total = term if total is None else total + term
        return total

    def tn(a, b):
        return lax.dot_general(a, b, (((0,), (0,)), ((), ())), preferred_element_type=jnp.float32)

    def body(group, carry):
        parity, slot = group // 2, (group % 2) * GROUP
        base = parity * 512 + slot
        sent = parity * SPAN + slot
        x = jnp.concatenate([gather_window(hs, base + i) for i in range(GROUP)], axis=0)
        center = x - jnp.mean(x, axis=-1, keepdims=True)
        inv_std = lax.rsqrt(jnp.mean(center * center, axis=-1, keepdims=True) + 1e-5)
        unit = center * inv_std
        normed = (unit * gain_row).astype(jnp.bfloat16)
        packed[...] = jnp.dot(normed, w_qkv[...], preferred_element_type=jnp.float32).astype(
            jnp.bfloat16
        )
        units = [(i, hg) for i in range(GROUP) for hg in range(4)]
        g_all = [gather_window(gs, base + i).astype(jnp.bfloat16) for i in range(GROUP)]
        outs = {}
        for first in range(0, len(units), BREADTH):
            batch = units[first : first + BREADTH]
            st = []
            for i, hg in batch:
                rows = slice(i * 64, i * 64 + 64)
                lo = hg * 128
                k = packed[rows, 512 + lo : 512 + lo + 128]
                v = packed[rows, 1024 + lo : 1024 + lo + 128]
                q_bd = spread(packed[rows, lo : lo + 128])
                g_bd = spread(g_all[i][:, lo : lo + 128])
                st.append((k, v, q_bd, g_bd))
            sd = [(nt(k, q_bd), nt(v, g_bd)) for k, v, q_bd, g_bd in st]
            soft = []
            for s, dp in sd:
                s = s * scale
                e = jnp.exp(s - jnp.max(s, axis=0, keepdims=True))
                p = e * (1.0 / jnp.sum(e, axis=0, keepdims=True))
                dot = jnp.sum(dp * p, axis=0, keepdims=True)
                soft.append((p.astype(jnp.bfloat16), (p * (dp - dot) * scale).astype(jnp.bfloat16)))
            prods = []
            for (k, v, q_bd, g_bd), (p, ds) in zip(st, soft):
                prods.append((
                    jnp.dot(p, g_bd, preferred_element_type=jnp.float32),
                    jnp.dot(ds, q_bd, preferred_element_type=jnp.float32),
                    tn(ds, k),
                    tn(p, v),
                ))
            for (i, hg), (dv, dk, dq, o) in zip(batch, prods):
                rows = slice(i * 64, i * 64 + 64)
                lo = hg * 128
                gpack[rows, lo : lo + 128] = collect(dq).astype(jnp.bfloat16)
                gpack[rows, 512 + lo : 512 + lo + 128] = dk.astype(jnp.bfloat16)
                gpack[rows, 1024 + lo : 1024 + lo + 128] = dv.astype(jnp.bfloat16)
                outs[i, hg] = collect(o)
        for i in range(GROUP):
            scatter_window(gs, base + i, jnp.concatenate([outs[i, hg] for hg in range(4)], axis=1))
        scaled = nt(gpack[...], w_qkv[...]) * gain_row
        grad = inv_std * (
            scaled
            - jnp.mean(scaled, axis=-1, keepdims=True)
            - unit * jnp.mean(scaled * unit, axis=-1, keepdims=True)
        )
        for i in range(GROUP):
            for c in range(4):
                sends[pl.ds(sent + i + c * 10, 64, stride=BLOCK_ROWS), :] = grad[
                    i * 64 : i * 64 + 64, lanes_of(c)
                ]
        return carry

    lax.fori_loop(0, WINDOWS // GROUP, body, 0)
    return_slots(place, sends)
    back_out[...] = sends[...].astype(jnp.bfloat16)
    for c in range(4):
        att_out[:, c * 128 : c * 128 + 128] = gs[c].astype(jnp.bfloat16)


def attend(place, hid, gatt, gain, w_qkv):
    blocks = (128 * BLOCK_ROWS, 128)
    return pl.pallas_call(
        attend_kernel,
        out_shape=(
            jax.ShapeDtypeStruct(blocks, jnp.bfloat16),
            jax.ShapeDtypeStruct(hid.shape, jnp.bfloat16),
        ),
        in_specs=[SMEM] + [VMEM] * 4,
        out_specs=(VMEM, VMEM),
        scratch_shapes=[
            pltpu.VMEM((4, 1024, 128), jnp.float32),
            pltpu.VMEM((4, 1024, 128), jnp.float32),
            pltpu.VMEM(blocks, jnp.float32),
            pltpu.VMEM((GROUP * 64, 1536), jnp.bfloat16),
            pltpu.VMEM((GROUP * 64, 1536), jnp.bfloat16),
        ],
        name="window_attention",
        compiler_params=pltpu.CompilerParams(vmem_limit_bytes=48 * 1024 * 1024),
    )(place, hid, gatt, gain, w_qkv)


def neighbour_pair(axis, size, to_next, to_prev):
    up = [(i, i + 1) for i in range(size - 1)]
    down = [(i + 1, i) for i in range(size - 1)]
    return lax.ppermute(to_next, axis, up), lax.ppermute(to_prev, axis, down)


def edge_columns(parts):
    rows = jnp.concatenate(parts, axis=0).transpose(1, 0, 2)
    rows = jnp.pad(rows, ((0, 0), (0, EDGE - rows.shape[1]), (0, 0)))
    return rows.reshape(-1, rows.shape[2])


EARLY = 5


def device_work(tokens, grad_output, w_exp, dw_kernel, w_proj, ln_gain, w_qkv, w_out):
    rows, cols, width = tokens.shape
    blocks = w_exp.shape[1] // BLK
    row_count = lax.axis_size("row")
    col_count = lax.axis_size("col")
    groups = [
        [
            (2 * q + h) * col_count + c
            for h in range(2)
            for q in range(row_count // 2)
            for c in range(col_count)
        ]
    ]
    row_at, col_at = lax.axis_index("row"), lax.axis_index("col")
    place = jnp.stack([row_at % 2, row_at // 2 * col_count + col_at]).astype(jnp.int32)

    def exchange(flat):
        sent = flat.reshape(row_count * col_count, -1, flat.shape[1])
        moved = lax.all_to_all(
            sent, ("row", "col"), split_axis=0, concat_axis=0, tiled=True,
            axis_index_groups=groups,
        )
        return moved.reshape(flat.shape)

    from_top, from_bot = neighbour_pair(
        "row",
        row_count,
        jnp.concatenate([tokens[rows - 2 :], grad_output[rows - 1 :]], axis=0),
        jnp.concatenate([tokens[:2], grad_output[:1]], axis=0),
    )
    top, g_top, bot, g_bot = from_top[:2], from_top[2:], from_bot[:2], from_bot[2:]
    grad_flat = grad_output.reshape(rows * cols, width)
    grad_att = grad_att_for_owners(place, grad_flat, w_out)

    near_right = edge_columns([x[:, cols - 2 :] for x in (top, tokens, bot)])
    near_left = edge_columns([x[:, :2] for x in (top, tokens, bot)])
    grad_right = edge_columns([x[:, cols - 1 :] for x in (g_top, grad_output, g_bot)])
    grad_left = edge_columns([x[:, :1] for x in (g_top, grad_output, g_bot)])
    to_right = jnp.concatenate([near_right, grad_right], axis=0)
    to_left = jnp.concatenate([near_left, grad_left], axis=0)
    to_right, to_left, grad_att = lax.optimization_barrier((to_right, to_left, grad_att))
    from_left, from_right = neighbour_pair("col", col_count, to_right, to_left)
    grad_win = exchange(grad_att)

    hidden, sent = forward(
        place, from_top, tokens, from_bot, from_left, from_right, w_exp, dw_kernel, w_proj
    )
    sent, grad_win = lax.optimization_barrier((sent, grad_win))
    hidden_win = exchange(sent)
    w_late, _ = lax.optimization_barrier((w_exp, sent))
    halo = (from_top, tokens, from_bot, from_left, near_left, near_right, from_right)
    tables = slopes(*halo, w_late, dw_kernel, 0, EARLY)
    hidden_win, *tables = lax.optimization_barrier((hidden_win, *tables))
    back_win, att_win = attend(place, hidden_win, grad_win, ln_gain.reshape(1, width), w_qkv)
    back = exchange(back_win)
    w_last, att_win = lax.optimization_barrier((w_exp, att_win))
    tables = slopes(*halo, w_last, dw_kernel, EARLY, blocks - EARLY, tables)
    attn_win = jnp.dot(att_win, w_out, preferred_element_type=jnp.float32).astype(jnp.bfloat16)
    back, attn_win, *tables = lax.optimization_barrier((back, attn_win, *tables))
    attn = exchange(attn_win)
    grad_tokens = backward(
        place, from_top, grad_flat, back, from_bot, from_left, from_right, tables,
        w_exp, dw_kernel, w_proj,
    )
    attn, grad_tokens = lax.optimization_barrier((attn, grad_tokens))
    output = finish(place, hidden, attn)
    return output.reshape(tokens.shape), grad_tokens.reshape(tokens.shape)


def solution(mesh):
    in_specs = (P("row", "col", None), P("row", "col", None), P(), P(), P(), P(), P(), P())
    out_specs = (P("row", "col", None), P("row", "col", None))
    return jax.shard_map(
        device_work, mesh=mesh, in_specs=in_specs, out_specs=out_specs, check_vma=False
    )
```

```python
import jax
import jax.numpy as jnp
from jax import lax
from jax.experimental import pallas as pl
from jax.experimental.pallas import tpu as pltpu
from jax.sharding import PartitionSpec as P


C0 = 0.7978845608028654
C1 = C0 * 0.044715
BLK = 256
FRAME = 80
EDGE = 24
LIMIT = 60 * 1024 * 1024


def half_gelu(h):
    h2 = h * h
    return h2, jnp.tanh(h * ((2.0 * C0) + (8.0 * C1) * h2))


def gelu_value(h, t):
    return h + h * t


def double_slope(h, h2, t):
    return (1.0 + t) + (1.0 - t * t) * (h * ((2.0 * C0) + (24.0 * C1) * h2))


def nt(a, b):
    return lax.dot_general(a, b, (((1,), (1,)), ((), ())), preferred_element_type=jnp.float32)


def round_f32(x):
    return x.astype(jnp.bfloat16).astype(jnp.float32)


def lanes_of(part):
    return slice(part * 128, part * 128 + 128)


def put_rows(dst, values, row, count):
    for part in range(BLK // 128):
        dst[part, row : row + count, 8:72, :] = values[:, lanes_of(part)].reshape(count, 64, 128)


def put_edge(dst, values, first, count, col):
    for part in range(BLK // 128):
        for r in range(count):
            dst[part, r, col : col + 1, :] = values[first + r : first + r + 1, lanes_of(part)]


def conv_row(src, part, row, taps):
    total = None
    for a in range(3):
        for b in range(3):
            term = src[part, row + a, 7 + b : 71 + b, :] * taps[a][b]
            total = term if total is None else total + term
    return total


def read_taps(dw, part, flip):
    taps = []
    for a in range(3):
        aa = 2 - a if flip else a
        order = (2, 1, 0) if flip else (0, 1, 2)
        taps.append([0.5 * dw[aa, b : b + 1, lanes_of(part)] for b in order])
    return taps


SLOTS = 8
BLOCK_ROWS = 40
SPAN = 64 * BLOCK_ROWS


def send_order(x, slot, parity):
    k = 8 * slot
    if k:
        x = jnp.concatenate([x[k:], x[:k]], axis=0)
    return jnp.where(parity == 1, pltpu.roll(x, 60, 0), x)


def receive_order(x, slot, parity):
    k = 8 * slot
    if k:
        x = jnp.concatenate([x[64 - k :], x[: 64 - k]], axis=0)
    return jnp.where(parity == 1, pltpu.roll(x, 4, 0), x)


def pack_for_owners(read, parity, packed_rows, out):
    for c in range(4):
        for row in range(16):
            x = send_order(read(row, lanes_of(c)), row % 8, parity)
            packed_rows[c, pl.ds(row // 8 * 512 + row % 8, 64, stride=SLOTS), :] = x
        out[:, lanes_of(c)] = packed_rows[c].astype(jnp.bfloat16)


def grad_att_kernel(place, grad, w_out, out, product, packed_rows):
    product[...] = nt(grad[...], w_out[...])
    pack_for_owners(
        lambda row, lanes: product[row * 64 : row * 64 + 64, lanes], place[0], packed_rows, out
    )


SMEM = pl.BlockSpec(memory_space=pltpu.SMEM)
VMEM = pl.BlockSpec(memory_space=pltpu.VMEM)


def grad_att_for_owners(place, grad, w_out):
    return pl.pallas_call(
        grad_att_kernel,
        out_shape=jax.ShapeDtypeStruct(grad.shape, jnp.bfloat16),
        in_specs=[SMEM, VMEM, VMEM],
        out_specs=VMEM,
        scratch_shapes=[
            pltpu.VMEM(grad.shape, jnp.float32),
            pltpu.VMEM((4, 1024, 128), jnp.float32),
        ],
        name="grad_att",
        compiler_params=pltpu.CompilerParams(vmem_limit_bytes=16 * 1024 * 1024),
    )(place, grad, w_out)


def finish_kernel(place, hidden, attn, out, rows_of):
    for c in range(4):
        rows_of[c] = attn[:, lanes_of(c)].astype(jnp.float32)
        for row in range(16):
            x = rows_of[c, pl.ds(row // 8 * 512 + row % 8, 64, stride=SLOTS), :]
            at = slice(row * 64, row * 64 + 64)
            total = hidden[at, lanes_of(c)].astype(jnp.float32) + receive_order(
                x, row % 8, place[0]
            )
            out[at, lanes_of(c)] = total.astype(jnp.bfloat16)


def finish(place, hidden, attn):
    return pl.pallas_call(
        finish_kernel,
        out_shape=jax.ShapeDtypeStruct(hidden.shape, jnp.bfloat16),
        in_specs=[SMEM, VMEM, VMEM],
        out_specs=VMEM,
        scratch_shapes=[pltpu.VMEM((4, 1024, 128), jnp.float32)],
        name="add_attention",
        compiler_params=pltpu.CompilerParams(vmem_limit_bytes=16 * 1024 * 1024),
    )(place, hidden, attn)


def fwd_kernel(place, top, mid, bot, left, right, w_exp, dw, w_proj, out, sent, act, acc, gout, packed_rows):
    step = pl.program_id(0)
    width = mid.shape[-1]
    w = w_exp[...] * jnp.bfloat16(0.5)

    @pl.when(step == 0)
    def _():
        acc[...] = mid[...].reshape(1024, width).astype(jnp.float32)

    def act_of(x):
        h = jnp.dot(x, w, preferred_element_type=jnp.float32)
        _, t = half_gelu(h)
        return round_f32(gelu_value(h, t))

    put_edge(act, act_of(left[: 2 * EDGE])[EDGE:], 1, 18, 7)
    put_edge(act, act_of(right[: 2 * EDGE])[:EDGE], 1, 18, 72)
    put_rows(act, act_of(top[1]), 0, 1)
    for r in range(0, 16, 4):
        put_rows(act, act_of(mid[r : r + 4].reshape(256, width)), 1 + r, 4)
    put_rows(act, act_of(bot[0]), 17, 1)

    for part in range(BLK // 128):
        taps = read_taps(dw, part, False)
        for r in range(16):
            h = conv_row(act, part, r, taps)
            _, t = half_gelu(h)
            gout[r * 64 : r * 64 + 64, lanes_of(part)] = gelu_value(h, t).astype(jnp.bfloat16)
    wp = w_proj[...]
    for r in range(0, 1024, 256):
        acc[r : r + 256] += jnp.dot(gout[r : r + 256], wp, preferred_element_type=jnp.float32)

    @pl.when(step == pl.num_programs(0) - 1)
    def _():
        out[...] = acc[...].astype(jnp.bfloat16)
        pack_for_owners(
            lambda row, lanes: acc[row * 64 : row * 64 + 64, lanes], place[0], packed_rows, sent
        )


def full(shape):
    return pl.BlockSpec(shape, lambda i: (0,) * len(shape))


def forward(place, top, mid, bot, left, right, w_exp, dw, w_proj):
    width, expand = w_exp.shape
    return pl.pallas_call(
        fwd_kernel,
        grid=(expand // BLK,),
        out_shape=(jax.ShapeDtypeStruct((1024, width), jnp.bfloat16),) * 2,
        in_specs=[
            SMEM, full(top.shape), full(mid.shape), full(bot.shape), full(left.shape),
            full(right.shape),
            pl.BlockSpec((width, BLK), lambda i: (0, i)),
            pl.BlockSpec((3, 3, BLK), lambda i: (0, 0, i)),
            pl.BlockSpec((BLK, width), lambda i: (i, 0)),
        ],
        out_specs=(full((1024, width)),) * 2,
        scratch_shapes=[
            pltpu.VMEM((BLK // 128, 18, FRAME, 128), jnp.float32),
            pltpu.VMEM((1024, width), jnp.float32),
            pltpu.VMEM((1024, BLK), jnp.bfloat16),
            pltpu.VMEM((4, 1024, 128), jnp.float32),
        ],
        name="mbconv_forward",
        compiler_params=pltpu.CompilerParams(vmem_limit_bytes=LIMIT),
    )(place, top, mid, bot, left, right, w_exp, dw, w_proj)


def slope_kernel(top, mid, bot, left, near_left, near_right, right, w_exp, dw, *rest):
    pre_out, conv_out, edge_out, act, cols = rest[-5:]
    width = mid.shape[-1]
    w = w_exp[...] * jnp.bfloat16(0.5)

    def act_of(x, slope_row=None):
        h = jnp.dot(x, w, preferred_element_type=jnp.float32)
        h2, t = half_gelu(h)
        if slope_row is not None:
            pre_out[slope_row * 64 : slope_row * 64 + x.shape[0], :] = double_slope(h, h2, t)
        return round_f32(gelu_value(h, t))

    for side, pair in enumerate((left, near_left, near_right, right)):
        a = act_of(pair[: 2 * EDGE])
        for part in range(BLK // 128):
            cols[part, 2 * side : 2 * side + 2, :, :] = a[:, lanes_of(part)].reshape(2, EDGE, 128)
        if side == 0:
            put_edge(act, a[EDGE:], 0, 20, 7)
        if side == 3:
            put_edge(act, a[:EDGE], 0, 20, 72)
    put_rows(act, act_of(top[:2].reshape(128, width)), 0, 2)
    for r in range(0, 16, 4):
        put_rows(act, act_of(mid[r : r + 4].reshape(256, width), r), 2 + r, 4)
    put_rows(act, act_of(bot[:2].reshape(128, width)), 18, 2)

    for part in range(BLK // 128):
        taps = read_taps(dw, part, False)
        for r in range(18):
            h = conv_row(act, part, r, taps)
            h2, t = half_gelu(h)
            conv_out[r * 64 : r * 64 + 64, lanes_of(part)] = double_slope(h, h2, t)
        for side in range(2):
            h = None
            for a in range(3):
                for b in range(3):
                    term = cols[part, 5 * side + b, a : a + 18, :] * taps[a][b]
                    h = term if h is None else h + term
            h2, t = half_gelu(h)
            edge_out[side * EDGE : side * EDGE + 18, lanes_of(part)] = double_slope(h, h2, t)
            edge_out[side * EDGE + 18 : side * EDGE + EDGE, lanes_of(part)] = jnp.zeros(
                (EDGE - 18, 128), jnp.float32
            )


def slopes(top, mid, bot, left, near_left, near_right, right, w_exp, dw, first, count, done=()):
    width, expand = w_exp.shape
    rows = (1024, 18 * 64, 2 * EDGE)
    operands = (top, mid, bot, left, near_left, near_right, right)
    return pl.pallas_call(
        slope_kernel,
        grid=(count,),
        out_shape=tuple(jax.ShapeDtypeStruct((n, expand), jnp.float32) for n in rows),
        in_specs=[
            *(full(x.shape) for x in operands),
            pl.BlockSpec((width, BLK), lambda i: (0, i + first)),
            pl.BlockSpec((3, 3, BLK), lambda i: (0, 0, i + first)),
            *(pl.BlockSpec(memory_space=pl.ANY) for _ in done),
        ],
        out_specs=tuple(pl.BlockSpec((n, BLK), lambda i: (0, i + first)) for n in rows),
        input_output_aliases={9 + i: i for i in range(len(done))},
        scratch_shapes=[
            pltpu.VMEM((BLK // 128, 20, FRAME, 128), jnp.float32),
            pltpu.VMEM((BLK // 128, 8, EDGE, 128), jnp.float32),
        ],
        name="mbconv_slopes",
        compiler_params=pltpu.CompilerParams(vmem_limit_bytes=LIMIT),
    )(*operands, w_exp, dw, *done)


def bwd_kernel(place, top, grad, back, bot, left, right, pre_slope, conv_slope, edge_slope,
               w_exp, dw, w_proj, out, mixed, pre, acc, rounded, got, ends, sides):
    step = pl.program_id(0)

    @pl.when(step == 0)
    def _():
        parity = place[0]
        got[...] = back[...].astype(jnp.float32)

        def tokens_of(half, slot, c):
            return got[pl.ds(half * SPAN + c * 10 + slot, 64, stride=BLOCK_ROWS), :]

        def token_of(half, shift, column, c):
            owner = (column + 128 - shift) & 63
            return got[pl.ds(half * SPAN + owner * BLOCK_ROWS + c * 10 + 9, 1), :]

        for c in range(4):
            lanes = lanes_of(c)
            for row in range(16):
                at = slice(row * 64, row * 64 + 64)
                x = receive_order(tokens_of(row // 8, row % 8, c), row % 8, parity)
                total = grad[at, lanes].astype(jnp.float32) + x
                acc[at, lanes] = total
                rounded[at, lanes] = total.astype(jnp.bfloat16)
            low = receive_order(tokens_of(0, 8, c), 0, 1 - parity)
            ends[64:128, lanes] = (bot[2, :, lanes].astype(jnp.float32) + low).astype(jnp.bfloat16)
            high = receive_order(tokens_of(1, 8, c), 7, 1 - parity)
            ends[0:64, lanes] = (top[2, :, lanes].astype(jnp.float32) + high).astype(jnp.bfloat16)
            for side, (halo, column) in enumerate(((left, 63), (right, 0))):
                sides[side, :, lanes] = halo[:, lanes].astype(jnp.float32)[2 * EDGE :]
                for i in range(18):
                    half, slot, flip = (i - 1) // 8, (i - 1) % 8, parity
                    if i == 0:
                        half, slot, flip = 1, 7, 1 - parity
                    if i == 17:
                        half, slot, flip = 0, 0, 1 - parity
                    sides[side, i : i + 1, lanes] += token_of(
                        half, 8 * slot + 4 * flip, column, c
                    )

    wp = w_proj[...] * jnp.bfloat16(0.5)
    for side, col in enumerate((7, 72)):
        edge = nt(sides[side].astype(jnp.bfloat16), wp)
        edge = edge * edge_slope[side * EDGE : side * EDGE + EDGE]
        put_edge(mixed, round_f32(edge), 0, 18, col)

    def put(x, row, count):
        mid = nt(x, wp) * conv_slope[row * 64 : (row + count) * 64]
        put_rows(mixed, round_f32(mid), row, count)

    put(ends[0:64], 0, 1)
    for r in range(0, 16, 4):
        put(rounded[r * 64 : r * 64 + 256], 1 + r, 4)
    put(ends[64:128], 17, 1)

    for part in range(BLK // 128):
        taps = read_taps(dw, part, True)
        for r in range(16):
            rows = slice(r * 64, r * 64 + 64)
            z = conv_row(mixed, part, r, taps) * pre_slope[rows, lanes_of(part)]
            pre[rows, lanes_of(part)] = z.astype(jnp.bfloat16)
    w = w_exp[...]
    for r in range(0, 1024, 256):
        acc[r : r + 256] += nt(pre[r : r + 256], w)

    @pl.when(step == pl.num_programs(0) - 1)
    def _():
        out[...] = acc[...].astype(jnp.bfloat16)


def backward(place, top, grad, back, bot, left, right, tables, w_exp, dw, w_proj):
    width, expand = w_exp.shape
    return pl.pallas_call(
        bwd_kernel,
        grid=(expand // BLK,),
        out_shape=jax.ShapeDtypeStruct((1024, width), jnp.bfloat16),
        in_specs=[
            SMEM, full(top.shape), full(grad.shape), full(back.shape), full(bot.shape),
            full(left.shape), full(right.shape),
            *(pl.BlockSpec((x.shape[0], BLK), lambda i: (0, i)) for x in tables),
            pl.BlockSpec((width, BLK), lambda i: (0, i)),
            pl.BlockSpec((3, 3, BLK), lambda i: (0, 0, i)),
            pl.BlockSpec((BLK, width), lambda i: (i, 0)),
        ],
        out_specs=full((1024, width)),
        scratch_shapes=[
            pltpu.VMEM((BLK // 128, 18, FRAME, 128), jnp.float32),
            pltpu.VMEM((1024, BLK), jnp.bfloat16),
            pltpu.VMEM((1024, width), jnp.float32),
            pltpu.VMEM((1024, width), jnp.bfloat16),
            pltpu.VMEM(back.shape, jnp.float32),
            pltpu.VMEM((128, width), jnp.bfloat16),
            pltpu.VMEM((2, EDGE, width), jnp.float32),
        ],
        name="mbconv_backward",
        compiler_params=pltpu.CompilerParams(vmem_limit_bytes=LIMIT),
    )(place, top, grad, back, bot, left, right, *tables, w_exp, dw, w_proj)


WINDOWS = 16
GROUP = 4
BREADTH = 8


def gather_window(src, start):
    return jnp.concatenate(
        [src[c, pl.ds(start, 64, stride=SLOTS), :] for c in range(4)], axis=1
    )


def scatter_window(dst, start, values):
    for c in range(4):
        dst[c, pl.ds(start, 64, stride=SLOTS), :] = values[:, lanes_of(c)]


def return_slots(place, dst):
    half, owner = place[0], place[1]
    member = lax.broadcasted_iota(jnp.int32, (64, 128), 0)
    for parity in range(2):
        other = 1 - parity
        edge_slot = 7 * half
        row_shift = 1 - half if parity == 1 else -half
        near = owner + 4 * parity
        at_left = (near & 7) == 0
        at_right = (near & 7) == 7
        column = (owner + 8 * edge_slot + 4 * other) & 63
        corner_left = column == 0
        corner_right = column == 63
        side = at_left | at_right
        line = jnp.where(at_left, (64 - near) >> 3, (127 - near) >> 3) & 7
        start = jnp.where(side, parity * SPAN + line, other * SPAN + edge_slot)
        rows_on = jnp.where(side, 0, row_shift)
        cols_on = jnp.where(at_left | corner_left, 1, -1)
        exists = side | corner_left | corner_right
        cases = (
            (8, other * SPAN + edge_slot, row_shift, 0, half >= 0),
            (9, start, rows_on, cols_on, exists),
        )
        for slot, begin, dq, dc, there in cases:
            q = (member >> 3) + dq
            c = (member & 7) + dc
            limit = jnp.where(there, 8, 0)
            valid = (q >= 0) & (q < limit) & (c >= 0) & (c < 8)
            shift = (64 - 8 * dq - dc) & 63
            for chunk in range(4):
                x = dst[pl.ds(begin + chunk * 10, 64, stride=BLOCK_ROWS), :]
                x = jnp.where(valid, pltpu.roll(x, shift, 0), 0.0)
                dst[pl.ds(parity * SPAN + chunk * 10 + slot, 64, stride=BLOCK_ROWS), :] = x


def attend_kernel(place, hid, gatt, gain, w_qkv, back_out, att_out, hs, gs, sends, packed, gpack):
    scale = 32 ** (-0.5)
    for c in range(4):
        hs[c] = hid[:, c * 128 : c * 128 + 128].astype(jnp.float32)
        gs[c] = gatt[:, c * 128 : c * 128 + 128].astype(jnp.float32)
    lane = lax.broadcasted_iota(jnp.int32, (64, 128), 1)
    masks = [(lane >= 32 * h) & (lane < 32 * h + 32) for h in range(4)]
    gain_row = gain[...]

    def spread(x):
        zero = jnp.zeros_like(x)
        return jnp.concatenate([jnp.where(m, x, zero) for m in masks], axis=0)

    def collect(y):
        total = None
        for h in range(4):
            term = jnp.where(masks[h], y[h * 64 : h * 64 + 64], 0.0)
            total = term if total is None else total + term
        return total

    def tn(a, b):
        return lax.dot_general(a, b, (((0,), (0,)), ((), ())), preferred_element_type=jnp.float32)

    def body(group, carry):
        parity, slot = group // 2, (group % 2) * GROUP
        base = parity * 512 + slot
        sent = parity * SPAN + slot
        x = jnp.concatenate([gather_window(hs, base + i) for i in range(GROUP)], axis=0)
        center = x - jnp.mean(x, axis=-1, keepdims=True)
        inv_std = lax.rsqrt(jnp.mean(center * center, axis=-1, keepdims=True) + 1e-5)
        unit = center * inv_std
        normed = (unit * gain_row).astype(jnp.bfloat16)
        packed[...] = jnp.dot(normed, w_qkv[...], preferred_element_type=jnp.float32).astype(
            jnp.bfloat16
        )
        units = [(i, hg) for i in range(GROUP) for hg in range(4)]
        g_all = [gather_window(gs, base + i).astype(jnp.bfloat16) for i in range(GROUP)]
        outs = {}
        for first in range(0, len(units), BREADTH):
            batch = units[first : first + BREADTH]
            st = []
            for i, hg in batch:
                rows = slice(i * 64, i * 64 + 64)
                lo = hg * 128
                k = packed[rows, 512 + lo : 512 + lo + 128]
                v = packed[rows, 1024 + lo : 1024 + lo + 128]
                q_bd = spread(packed[rows, lo : lo + 128])
                g_bd = spread(g_all[i][:, lo : lo + 128])
                st.append((k, v, q_bd, g_bd))
            sd = [(nt(k, q_bd), nt(v, g_bd)) for k, v, q_bd, g_bd in st]
            soft = []
            for s, dp in sd:
                s = s * scale
                e = jnp.exp(s - jnp.max(s, axis=0, keepdims=True))
                p = e * (1.0 / jnp.sum(e, axis=0, keepdims=True))
                dot = jnp.sum(dp * p, axis=0, keepdims=True)
                soft.append((p.astype(jnp.bfloat16), (p * (dp - dot) * scale).astype(jnp.bfloat16)))
            prods = []
            for (k, v, q_bd, g_bd), (p, ds) in zip(st, soft):
                prods.append((
                    jnp.dot(p, g_bd, preferred_element_type=jnp.float32),
                    jnp.dot(ds, q_bd, preferred_element_type=jnp.float32),
                    tn(ds, k),
                    tn(p, v),
                ))
            for (i, hg), (dv, dk, dq, o) in zip(batch, prods):
                rows = slice(i * 64, i * 64 + 64)
                lo = hg * 128
                gpack[rows, lo : lo + 128] = collect(dq).astype(jnp.bfloat16)
                gpack[rows, 512 + lo : 512 + lo + 128] = dk.astype(jnp.bfloat16)
                gpack[rows, 1024 + lo : 1024 + lo + 128] = dv.astype(jnp.bfloat16)
                outs[i, hg] = collect(o)
        for i in range(GROUP):
            scatter_window(gs, base + i, jnp.concatenate([outs[i, hg] for hg in range(4)], axis=1))
        scaled = nt(gpack[...], w_qkv[...]) * gain_row
        grad = inv_std * (
            scaled
            - jnp.mean(scaled, axis=-1, keepdims=True)
            - unit * jnp.mean(scaled * unit, axis=-1, keepdims=True)
        )
        for i in range(GROUP):
            for c in range(4):
                sends[pl.ds(sent + i + c * 10, 64, stride=BLOCK_ROWS), :] = grad[
                    i * 64 : i * 64 + 64, lanes_of(c)
                ]
        return carry

    lax.fori_loop(0, WINDOWS // GROUP, body, 0)
    return_slots(place, sends)
    back_out[...] = sends[...].astype(jnp.bfloat16)
    for c in range(4):
        att_out[:, c * 128 : c * 128 + 128] = gs[c].astype(jnp.bfloat16)


def attend(place, hid, gatt, gain, w_qkv):
    blocks = (128 * BLOCK_ROWS, 128)
    return pl.pallas_call(
        attend_kernel,
        out_shape=(
            jax.ShapeDtypeStruct(blocks, jnp.bfloat16),
            jax.ShapeDtypeStruct(hid.shape, jnp.bfloat16),
        ),
        in_specs=[SMEM] + [VMEM] * 4,
        out_specs=(VMEM, VMEM),
        scratch_shapes=[
            pltpu.VMEM((4, 1024, 128), jnp.float32),
            pltpu.VMEM((4, 1024, 128), jnp.float32),
            pltpu.VMEM(blocks, jnp.float32),
            pltpu.VMEM((GROUP * 64, 1536), jnp.bfloat16),
            pltpu.VMEM((GROUP * 64, 1536), jnp.bfloat16),
        ],
        name="window_attention",
        compiler_params=pltpu.CompilerParams(vmem_limit_bytes=48 * 1024 * 1024),
    )(place, hid, gatt, gain, w_qkv)


def neighbour_pair(axis, size, to_next, to_prev):
    up = [(i, i + 1) for i in range(size - 1)]
    down = [(i + 1, i) for i in range(size - 1)]
    return lax.ppermute(to_next, axis, up), lax.ppermute(to_prev, axis, down)


def edge_columns(parts):
    rows = jnp.concatenate(parts, axis=0).transpose(1, 0, 2)
    rows = jnp.pad(rows, ((0, 0), (0, EDGE - rows.shape[1]), (0, 0)))
    return rows.reshape(-1, rows.shape[2])


EARLY = 5


def device_work(tokens, grad_output, w_exp, dw_kernel, w_proj, ln_gain, w_qkv, w_out):
    rows, cols, width = tokens.shape
    blocks = w_exp.shape[1] // BLK
    row_count = lax.axis_size("row")
    col_count = lax.axis_size("col")
    groups = [
        [
            (2 * q + h) * col_count + c
            for h in range(2)
            for q in range(row_count // 2)
            for c in range(col_count)
        ]
    ]
    row_at, col_at = lax.axis_index("row"), lax.axis_index("col")
    place = jnp.stack([row_at % 2, row_at // 2 * col_count + col_at]).astype(jnp.int32)

    def exchange(flat):
        sent = flat.reshape(row_count * col_count, -1, flat.shape[1])
        moved = lax.all_to_all(
            sent, ("row", "col"), split_axis=0, concat_axis=0, tiled=True,
            axis_index_groups=groups,
        )
        return moved.reshape(flat.shape)

    from_top, from_bot = neighbour_pair(
        "row",
        row_count,
        jnp.concatenate([tokens[rows - 2 :], grad_output[rows - 1 :]], axis=0),
        jnp.concatenate([tokens[:2], grad_output[:1]], axis=0),
    )
    top, g_top, bot, g_bot = from_top[:2], from_top[2:], from_bot[:2], from_bot[2:]
    grad_flat = grad_output.reshape(rows * cols, width)
    grad_att = grad_att_for_owners(place, grad_flat, w_out)

    near_right = edge_columns([x[:, cols - 2 :] for x in (top, tokens, bot)])
    near_left = edge_columns([x[:, :2] for x in (top, tokens, bot)])
    grad_right = edge_columns([x[:, cols - 1 :] for x in (g_top, grad_output, g_bot)])
    grad_left = edge_columns([x[:, :1] for x in (g_top, grad_output, g_bot)])
    to_right = jnp.concatenate([near_right, grad_right], axis=0)
    to_left = jnp.concatenate([near_left, grad_left], axis=0)
    to_right, to_left, grad_att = lax.optimization_barrier((to_right, to_left, grad_att))
    from_left, from_right = neighbour_pair("col", col_count, to_right, to_left)
    grad_win = exchange(grad_att)

    hidden, sent = forward(
        place, from_top, tokens, from_bot, from_left, from_right, w_exp, dw_kernel, w_proj
    )
    sent, grad_win = lax.optimization_barrier((sent, grad_win))
    hidden_win = exchange(sent)
    w_late, _ = lax.optimization_barrier((w_exp, sent))
    halo = (from_top, tokens, from_bot, from_left, near_left, near_right, from_right)
    tables = slopes(*halo, w_late, dw_kernel, 0, EARLY)
    hidden_win, *tables = lax.optimization_barrier((hidden_win, *tables))
    back_win, att_win = attend(place, hidden_win, grad_win, ln_gain.reshape(1, width), w_qkv)
    back = exchange(back_win)
    w_last, att_win = lax.optimization_barrier((w_exp, att_win))
    tables = slopes(*halo, w_last, dw_kernel, EARLY, blocks - EARLY, tables)
    attn_win = jnp.dot(att_win, w_out, preferred_element_type=jnp.float32).astype(jnp.bfloat16)
    back, attn_win, *tables = lax.optimization_barrier((back, attn_win, *tables))
    attn = exchange(attn_win)
    grad_tokens = backward(
        place, from_top, grad_flat, back, from_bot, from_left, from_right, tables,
        w_exp, dw_kernel, w_proj,
    )
    attn, grad_tokens = lax.optimization_barrier((attn, grad_tokens))
    output = finish(place, hidden, attn)
    return output.reshape(tokens.shape), grad_tokens.reshape(tokens.shape)


def solution(mesh):
    in_specs = (P("row", "col", None), P("row", "col", None), P(), P(), P(), P(), P(), P())
    out_specs = (P("row", "col", None), P("row", "col", None))
    return jax.shard_map(
        device_work, mesh=mesh, in_specs=in_specs, out_specs=out_specs, check_vma=False
    )
```

```python
import jax
import jax.numpy as jnp
from jax import lax
from jax.experimental import pallas as pl
from jax.experimental.pallas import tpu as pltpu
from jax.sharding import PartitionSpec as P


C0 = 0.7978845608028654
C1 = C0 * 0.044715
BLK = 256
WIDE = 512
FRAME = 80
EDGE = 24
LIMIT = 60 * 1024 * 1024


def half_gelu(h):
    h2 = h * h
    return h2, jnp.tanh(h * ((2.0 * C0) + (8.0 * C1) * h2))


def gelu_value(h, t):
    return h + h * t


def double_slope(h, h2, t):
    return (1.0 + t) + (1.0 - t * t) * (h * ((2.0 * C0) + (24.0 * C1) * h2))


def nt(a, b):
    return lax.dot_general(a, b, (((1,), (1,)), ((), ())), preferred_element_type=jnp.float32)


def round_f32(x):
    return x.astype(jnp.bfloat16).astype(jnp.float32)


def lanes_of(part):
    return slice(part * 128, part * 128 + 128)


def put_rows(dst, values, row, count):
    for part in range(values.shape[1] // 128):
        dst[part, row : row + count, 8:72, :] = values[:, lanes_of(part)].reshape(count, 64, 128)


def put_edge(dst, values, first, count, col):
    for part in range(values.shape[1] // 128):
        for r in range(count):
            dst[part, r, col : col + 1, :] = values[first + r : first + r + 1, lanes_of(part)]


def conv_row(src, part, row, taps):
    total = None
    for a in range(3):
        for b in range(3):
            term = src[part, row + a, 7 + b : 71 + b, :] * taps[a][b]
            total = term if total is None else total + term
    return total


def read_taps(dw, part, flip):
    taps = []
    for a in range(3):
        aa = 2 - a if flip else a
        order = (2, 1, 0) if flip else (0, 1, 2)
        taps.append([0.5 * dw[aa, b : b + 1, lanes_of(part)] for b in order])
    return taps


SLOTS = 8
BLOCK_ROWS = 40
SPAN = 64 * BLOCK_ROWS


def send_order(x, slot, parity):
    k = 8 * slot
    if k:
        x = jnp.concatenate([x[k:], x[:k]], axis=0)
    return jnp.where(parity == 1, pltpu.roll(x, 60, 0), x)


def receive_order(x, slot, parity):
    k = 8 * slot
    if k:
        x = jnp.concatenate([x[64 - k :], x[: 64 - k]], axis=0)
    return jnp.where(parity == 1, pltpu.roll(x, 4, 0), x)


def pack_for_owners(read, parity, packed_rows, out):
    for c in range(4):
        for row in range(16):
            x = send_order(read(row, lanes_of(c)), row % 8, parity)
            packed_rows[c, pl.ds(row // 8 * 512 + row % 8, 64, stride=SLOTS), :] = x
        out[:, lanes_of(c)] = packed_rows[c].astype(jnp.bfloat16)


def grad_att_kernel(place, grad, w_out, out, product, packed_rows):
    product[...] = nt(grad[...], w_out[...])
    pack_for_owners(
        lambda row, lanes: product[row * 64 : row * 64 + 64, lanes], place[0], packed_rows, out
    )


SMEM = pl.BlockSpec(memory_space=pltpu.SMEM)
VMEM = pl.BlockSpec(memory_space=pltpu.VMEM)


def grad_att_for_owners(place, grad, w_out):
    return pl.pallas_call(
        grad_att_kernel,
        out_shape=jax.ShapeDtypeStruct(grad.shape, jnp.bfloat16),
        in_specs=[SMEM, VMEM, VMEM],
        out_specs=VMEM,
        scratch_shapes=[
            pltpu.VMEM(grad.shape, jnp.float32),
            pltpu.VMEM((4, 1024, 128), jnp.float32),
        ],
        name="grad_att",
        compiler_params=pltpu.CompilerParams(vmem_limit_bytes=16 * 1024 * 1024),
    )(place, grad, w_out)


def finish_kernel(place, hidden, attn, out, rows_of):
    for c in range(4):
        rows_of[c] = attn[:, lanes_of(c)].astype(jnp.float32)
        for row in range(16):
            x = rows_of[c, pl.ds(row // 8 * 512 + row % 8, 64, stride=SLOTS), :]
            at = slice(row * 64, row * 64 + 64)
            total = hidden[at, lanes_of(c)].astype(jnp.float32) + receive_order(
                x, row % 8, place[0]
            )
            out[at, lanes_of(c)] = total.astype(jnp.bfloat16)


def finish(place, hidden, attn):
    return pl.pallas_call(
        finish_kernel,
        out_shape=jax.ShapeDtypeStruct(hidden.shape, jnp.bfloat16),
        in_specs=[SMEM, VMEM, VMEM],
        out_specs=VMEM,
        scratch_shapes=[pltpu.VMEM((4, 1024, 128), jnp.float32)],
        name="add_attention",
        compiler_params=pltpu.CompilerParams(vmem_limit_bytes=16 * 1024 * 1024),
    )(place, hidden, attn)


def fwd_kernel(place, top, mid, bot, left, right, w_exp, dw, w_proj, out, sent, act, acc, gout, packed_rows):
    step = pl.program_id(0)
    width = mid.shape[-1]
    w = w_exp[...] * jnp.bfloat16(0.5)

    @pl.when(step == 0)
    def _():
        acc[...] = mid[...].reshape(1024, width).astype(jnp.float32)

    def act_of(x):
        h = jnp.dot(x, w, preferred_element_type=jnp.float32)
        _, t = half_gelu(h)
        return round_f32(gelu_value(h, t))

    put_edge(act, act_of(left[: 2 * EDGE])[EDGE:], 1, 18, 7)
    put_edge(act, act_of(right[: 2 * EDGE])[:EDGE], 1, 18, 72)
    put_rows(act, act_of(top[1]), 0, 1)
    for r in range(0, 16, 4):
        put_rows(act, act_of(mid[r : r + 4].reshape(256, width)), 1 + r, 4)
    put_rows(act, act_of(bot[0]), 17, 1)

    for part in range(WIDE // 128):
        taps = read_taps(dw, part, False)
        for r in range(16):
            h = conv_row(act, part, r, taps)
            _, t = half_gelu(h)
            gout[r * 64 : r * 64 + 64, lanes_of(part)] = gelu_value(h, t).astype(jnp.bfloat16)
    wp = w_proj[...]
    for r in range(0, 1024, 256):
        acc[r : r + 256] += jnp.dot(gout[r : r + 256], wp, preferred_element_type=jnp.float32)

    @pl.when(step == pl.num_programs(0) - 1)
    def _():
        out[...] = acc[...].astype(jnp.bfloat16)
        pack_for_owners(
            lambda row, lanes: acc[row * 64 : row * 64 + 64, lanes], place[0], packed_rows, sent
        )


def full(shape):
    return pl.BlockSpec(shape, lambda i: (0,) * len(shape))


def forward(place, top, mid, bot, left, right, w_exp, dw, w_proj):
    width, expand = w_exp.shape
    return pl.pallas_call(
        fwd_kernel,
        grid=(expand // WIDE,),
        out_shape=(jax.ShapeDtypeStruct((1024, width), jnp.bfloat16),) * 2,
        in_specs=[
            SMEM, full(top.shape), full(mid.shape), full(bot.shape), full(left.shape),
            full(right.shape),
            pl.BlockSpec((width, WIDE), lambda i: (0, i)),
            pl.BlockSpec((3, 3, WIDE), lambda i: (0, 0, i)),
            pl.BlockSpec((WIDE, width), lambda i: (i, 0)),
        ],
        out_specs=(full((1024, width)),) * 2,
        scratch_shapes=[
            pltpu.VMEM((WIDE // 128, 18, FRAME, 128), jnp.float32),
            pltpu.VMEM((1024, width), jnp.float32),
            pltpu.VMEM((1024, WIDE), jnp.bfloat16),
            pltpu.VMEM((4, 1024, 128), jnp.float32),
        ],
        name="mbconv_forward",
        compiler_params=pltpu.CompilerParams(vmem_limit_bytes=LIMIT),
    )(place, top, mid, bot, left, right, w_exp, dw, w_proj)


def slope_kernel(top, mid, bot, left, near_left, near_right, right, w_exp, dw, *rest):
    pre_out, conv_out, edge_out, act, cols = rest[-5:]
    width = mid.shape[-1]
    w = w_exp[...] * jnp.bfloat16(0.5)

    def act_of(x, slope_row=None):
        h = jnp.dot(x, w, preferred_element_type=jnp.float32)
        h2, t = half_gelu(h)
        if slope_row is not None:
            pre_out[slope_row * 64 : slope_row * 64 + x.shape[0], :] = double_slope(h, h2, t)
        return round_f32(gelu_value(h, t))

    for side, pair in enumerate((left, near_left, near_right, right)):
        a = act_of(pair[: 2 * EDGE])
        for part in range(BLK // 128):
            cols[part, 2 * side : 2 * side + 2, :, :] = a[:, lanes_of(part)].reshape(2, EDGE, 128)
        if side == 0:
            put_edge(act, a[EDGE:], 0, 20, 7)
        if side == 3:
            put_edge(act, a[:EDGE], 0, 20, 72)
    put_rows(act, act_of(top[:2].reshape(128, width)), 0, 2)
    for r in range(0, 16, 4):
        put_rows(act, act_of(mid[r : r + 4].reshape(256, width), r), 2 + r, 4)
    put_rows(act, act_of(bot[:2].reshape(128, width)), 18, 2)

    for part in range(BLK // 128):
        taps = read_taps(dw, part, False)
        for r in range(18):
            h = conv_row(act, part, r, taps)
            h2, t = half_gelu(h)
            conv_out[r * 64 : r * 64 + 64, lanes_of(part)] = double_slope(h, h2, t)
        for side in range(2):
            h = None
            for a in range(3):
                for b in range(3):
                    term = cols[part, 5 * side + b, a : a + 18, :] * taps[a][b]
                    h = term if h is None else h + term
            h2, t = half_gelu(h)
            edge_out[side * EDGE : side * EDGE + 18, lanes_of(part)] = double_slope(h, h2, t)
            edge_out[side * EDGE + 18 : side * EDGE + EDGE, lanes_of(part)] = jnp.zeros(
                (EDGE - 18, 128), jnp.float32
            )


def slopes(top, mid, bot, left, near_left, near_right, right, w_exp, dw, first, count, done=()):
    width, expand = w_exp.shape
    rows = (1024, 18 * 64, 2 * EDGE)
    operands = (top, mid, bot, left, near_left, near_right, right)
    return pl.pallas_call(
        slope_kernel,
        grid=(count,),
        out_shape=tuple(jax.ShapeDtypeStruct((n, expand), jnp.float32) for n in rows),
        in_specs=[
            *(full(x.shape) for x in operands),
            pl.BlockSpec((width, BLK), lambda i: (0, i + first)),
            pl.BlockSpec((3, 3, BLK), lambda i: (0, 0, i + first)),
            *(pl.BlockSpec(memory_space=pl.ANY) for _ in done),
        ],
        out_specs=tuple(pl.BlockSpec((n, BLK), lambda i: (0, i + first)) for n in rows),
        input_output_aliases={9 + i: i for i in range(len(done))},
        scratch_shapes=[
            pltpu.VMEM((BLK // 128, 20, FRAME, 128), jnp.float32),
            pltpu.VMEM((BLK // 128, 8, EDGE, 128), jnp.float32),
        ],
        name="mbconv_slopes",
        compiler_params=pltpu.CompilerParams(vmem_limit_bytes=LIMIT),
    )(*operands, w_exp, dw, *done)


def bwd_kernel(place, top, grad, back, bot, left, right, pre_slope, conv_slope, edge_slope,
               w_exp, dw, w_proj, out, mixed, pre, acc, rounded, got, ends, sides):
    step = pl.program_id(0)

    @pl.when(step == 0)
    def _():
        parity = place[0]
        got[...] = back[...].astype(jnp.float32)

        def tokens_of(half, slot, c):
            return got[pl.ds(half * SPAN + c * 10 + slot, 64, stride=BLOCK_ROWS), :]

        def token_of(half, shift, column, c):
            owner = (column + 128 - shift) & 63
            return got[pl.ds(half * SPAN + owner * BLOCK_ROWS + c * 10 + 9, 1), :]

        for c in range(4):
            lanes = lanes_of(c)
            for row in range(16):
                at = slice(row * 64, row * 64 + 64)
                x = receive_order(tokens_of(row // 8, row % 8, c), row % 8, parity)
                total = grad[at, lanes].astype(jnp.float32) + x
                acc[at, lanes] = total
                rounded[at, lanes] = total.astype(jnp.bfloat16)
            low = receive_order(tokens_of(0, 8, c), 0, 1 - parity)
            ends[64:128, lanes] = (bot[2, :, lanes].astype(jnp.float32) + low).astype(jnp.bfloat16)
            high = receive_order(tokens_of(1, 8, c), 7, 1 - parity)
            ends[0:64, lanes] = (top[2, :, lanes].astype(jnp.float32) + high).astype(jnp.bfloat16)
            for side, (halo, column) in enumerate(((left, 63), (right, 0))):
                sides[side, :, lanes] = halo[:, lanes].astype(jnp.float32)[2 * EDGE :]
                for i in range(18):
                    half, slot, flip = (i - 1) // 8, (i - 1) % 8, parity
                    if i == 0:
                        half, slot, flip = 1, 7, 1 - parity
                    if i == 17:
                        half, slot, flip = 0, 0, 1 - parity
                    sides[side, i : i + 1, lanes] += token_of(
                        half, 8 * slot + 4 * flip, column, c
                    )

    wp = w_proj[...] * jnp.bfloat16(0.5)
    for side, col in enumerate((7, 72)):
        edge = nt(sides[side].astype(jnp.bfloat16), wp)
        edge = edge * edge_slope[side * EDGE : side * EDGE + EDGE]
        put_edge(mixed, round_f32(edge), 0, 18, col)

    def put(x, row, count):
        mid = nt(x, wp) * conv_slope[row * 64 : (row + count) * 64]
        put_rows(mixed, round_f32(mid), row, count)

    put(ends[0:64], 0, 1)
    for r in range(0, 16, 4):
        put(rounded[r * 64 : r * 64 + 256], 1 + r, 4)
    put(ends[64:128], 17, 1)

    for part in range(WIDE // 128):
        taps = read_taps(dw, part, True)
        for r in range(16):
            rows = slice(r * 64, r * 64 + 64)
            z = conv_row(mixed, part, r, taps) * pre_slope[rows, lanes_of(part)]
            pre[rows, lanes_of(part)] = z.astype(jnp.bfloat16)
    w = w_exp[...]
    for r in range(0, 1024, 256):
        acc[r : r + 256] += nt(pre[r : r + 256], w)

    @pl.when(step == pl.num_programs(0) - 1)
    def _():
        out[...] = acc[...].astype(jnp.bfloat16)


def backward(place, top, grad, back, bot, left, right, tables, w_exp, dw, w_proj):
    width, expand = w_exp.shape
    return pl.pallas_call(
        bwd_kernel,
        grid=(expand // WIDE,),
        out_shape=jax.ShapeDtypeStruct((1024, width), jnp.bfloat16),
        in_specs=[
            SMEM, full(top.shape), full(grad.shape), full(back.shape), full(bot.shape),
            full(left.shape), full(right.shape),
            *(pl.BlockSpec((x.shape[0], WIDE), lambda i: (0, i)) for x in tables),
            pl.BlockSpec((width, WIDE), lambda i: (0, i)),
            pl.BlockSpec((3, 3, WIDE), lambda i: (0, 0, i)),
            pl.BlockSpec((WIDE, width), lambda i: (i, 0)),
        ],
        out_specs=full((1024, width)),
        scratch_shapes=[
            pltpu.VMEM((WIDE // 128, 18, FRAME, 128), jnp.float32),
            pltpu.VMEM((1024, WIDE), jnp.bfloat16),
            pltpu.VMEM((1024, width), jnp.float32),
            pltpu.VMEM((1024, width), jnp.bfloat16),
            pltpu.VMEM(back.shape, jnp.float32),
            pltpu.VMEM((128, width), jnp.bfloat16),
            pltpu.VMEM((2, EDGE, width), jnp.float32),
        ],
        name="mbconv_backward",
        compiler_params=pltpu.CompilerParams(vmem_limit_bytes=LIMIT),
    )(place, top, grad, back, bot, left, right, *tables, w_exp, dw, w_proj)


WINDOWS = 16
GROUP = 4
BREADTH = 8


def gather_window(src, start):
    return jnp.concatenate(
        [src[c, pl.ds(start, 64, stride=SLOTS), :] for c in range(4)], axis=1
    )


def scatter_window(dst, start, values):
    for c in range(4):
        dst[c, pl.ds(start, 64, stride=SLOTS), :] = values[:, lanes_of(c)]


def return_slots(place, dst):
    half, owner = place[0], place[1]
    member = lax.broadcasted_iota(jnp.int32, (64, 128), 0)
    for parity in range(2):
        other = 1 - parity
        edge_slot = 7 * half
        row_shift = 1 - half if parity == 1 else -half
        near = owner + 4 * parity
        at_left = (near & 7) == 0
        at_right = (near & 7) == 7
        column = (owner + 8 * edge_slot + 4 * other) & 63
        corner_left = column == 0
        corner_right = column == 63
        side = at_left | at_right
        line = jnp.where(at_left, (64 - near) >> 3, (127 - near) >> 3) & 7
        start = jnp.where(side, parity * SPAN + line, other * SPAN + edge_slot)
        rows_on = jnp.where(side, 0, row_shift)
        cols_on = jnp.where(at_left | corner_left, 1, -1)
        exists = side | corner_left | corner_right
        cases = (
            (8, other * SPAN + edge_slot, row_shift, 0, half >= 0),
            (9, start, rows_on, cols_on, exists),
        )
        for slot, begin, dq, dc, there in cases:
            q = (member >> 3) + dq
            c = (member & 7) + dc
            limit = jnp.where(there, 8, 0)
            valid = (q >= 0) & (q < limit) & (c >= 0) & (c < 8)
            shift = (64 - 8 * dq - dc) & 63
            for chunk in range(4):
                x = dst[pl.ds(begin + chunk * 10, 64, stride=BLOCK_ROWS), :]
                x = jnp.where(valid, pltpu.roll(x, shift, 0), 0.0)
                dst[pl.ds(parity * SPAN + chunk * 10 + slot, 64, stride=BLOCK_ROWS), :] = x


def attend_kernel(place, hid, gatt, gain, w_qkv, back_out, att_out, hs, gs, sends, packed, gpack):
    scale = 32 ** (-0.5)
    for c in range(4):
        hs[c] = hid[:, c * 128 : c * 128 + 128].astype(jnp.float32)
        gs[c] = gatt[:, c * 128 : c * 128 + 128].astype(jnp.float32)
    lane = lax.broadcasted_iota(jnp.int32, (64, 128), 1)
    masks = [(lane >= 32 * h) & (lane < 32 * h + 32) for h in range(4)]
    gain_row = gain[...]

    def spread(x):
        zero = jnp.zeros_like(x)
        return jnp.concatenate([jnp.where(m, x, zero) for m in masks], axis=0)

    def collect(y):
        total = None
        for h in range(4):
            term = jnp.where(masks[h], y[h * 64 : h * 64 + 64], 0.0)
            total = term if total is None else total + term
        return total

    def tn(a, b):
        return lax.dot_general(a, b, (((0,), (0,)), ((), ())), preferred_element_type=jnp.float32)

    def body(group, carry):
        parity, slot = group // 2, (group % 2) * GROUP
        base = parity * 512 + slot
        sent = parity * SPAN + slot
        x = jnp.concatenate([gather_window(hs, base + i) for i in range(GROUP)], axis=0)
        center = x - jnp.mean(x, axis=-1, keepdims=True)
        inv_std = lax.rsqrt(jnp.mean(center * center, axis=-1, keepdims=True) + 1e-5)
        unit = center * inv_std
        normed = (unit * gain_row).astype(jnp.bfloat16)
        packed[...] = jnp.dot(normed, w_qkv[...], preferred_element_type=jnp.float32).astype(
            jnp.bfloat16
        )
        units = [(i, hg) for i in range(GROUP) for hg in range(4)]
        g_all = [gather_window(gs, base + i).astype(jnp.bfloat16) for i in range(GROUP)]
        outs = {}
        for first in range(0, len(units), BREADTH):
            batch = units[first : first + BREADTH]
            st = []
            for i, hg in batch:
                rows = slice(i * 64, i * 64 + 64)
                lo = hg * 128
                k = packed[rows, 512 + lo : 512 + lo + 128]
                v = packed[rows, 1024 + lo : 1024 + lo + 128]
                q_bd = spread(packed[rows, lo : lo + 128])
                g_bd = spread(g_all[i][:, lo : lo + 128])
                st.append((k, v, q_bd, g_bd))
            sd = [(nt(k, q_bd), nt(v, g_bd)) for k, v, q_bd, g_bd in st]
            soft = []
            for s, dp in sd:
                s = s * scale
                e = jnp.exp(s - jnp.max(s, axis=0, keepdims=True))
                p = e * (1.0 / jnp.sum(e, axis=0, keepdims=True))
                dot = jnp.sum(dp * p, axis=0, keepdims=True)
                soft.append((p.astype(jnp.bfloat16), (p * (dp - dot) * scale).astype(jnp.bfloat16)))
            prods = []
            for (k, v, q_bd, g_bd), (p, ds) in zip(st, soft):
                prods.append((
                    jnp.dot(p, g_bd, preferred_element_type=jnp.float32),
                    jnp.dot(ds, q_bd, preferred_element_type=jnp.float32),
                    tn(ds, k),
                    tn(p, v),
                ))
            for (i, hg), (dv, dk, dq, o) in zip(batch, prods):
                rows = slice(i * 64, i * 64 + 64)
                lo = hg * 128
                gpack[rows, lo : lo + 128] = collect(dq).astype(jnp.bfloat16)
                gpack[rows, 512 + lo : 512 + lo + 128] = dk.astype(jnp.bfloat16)
                gpack[rows, 1024 + lo : 1024 + lo + 128] = dv.astype(jnp.bfloat16)
                outs[i, hg] = collect(o)
        for i in range(GROUP):
            scatter_window(gs, base + i, jnp.concatenate([outs[i, hg] for hg in range(4)], axis=1))
        scaled = nt(gpack[...], w_qkv[...]) * gain_row
        grad = inv_std * (
            scaled
            - jnp.mean(scaled, axis=-1, keepdims=True)
            - unit * jnp.mean(scaled * unit, axis=-1, keepdims=True)
        )
        for i in range(GROUP):
            for c in range(4):
                sends[pl.ds(sent + i + c * 10, 64, stride=BLOCK_ROWS), :] = grad[
                    i * 64 : i * 64 + 64, lanes_of(c)
                ]
        return carry

    lax.fori_loop(0, WINDOWS // GROUP, body, 0)
    return_slots(place, sends)
    back_out[...] = sends[...].astype(jnp.bfloat16)
    for c in range(4):
        att_out[:, c * 128 : c * 128 + 128] = gs[c].astype(jnp.bfloat16)


def attend(place, hid, gatt, gain, w_qkv):
    blocks = (128 * BLOCK_ROWS, 128)
    return pl.pallas_call(
        attend_kernel,
        out_shape=(
            jax.ShapeDtypeStruct(blocks, jnp.bfloat16),
            jax.ShapeDtypeStruct(hid.shape, jnp.bfloat16),
        ),
        in_specs=[SMEM] + [VMEM] * 4,
        out_specs=(VMEM, VMEM),
        scratch_shapes=[
            pltpu.VMEM((4, 1024, 128), jnp.float32),
            pltpu.VMEM((4, 1024, 128), jnp.float32),
            pltpu.VMEM(blocks, jnp.float32),
            pltpu.VMEM((GROUP * 64, 1536), jnp.bfloat16),
            pltpu.VMEM((GROUP * 64, 1536), jnp.bfloat16),
        ],
        name="window_attention",
        compiler_params=pltpu.CompilerParams(vmem_limit_bytes=48 * 1024 * 1024),
    )(place, hid, gatt, gain, w_qkv)


def neighbour_pair(axis, size, to_next, to_prev):
    up = [(i, i + 1) for i in range(size - 1)]
    down = [(i + 1, i) for i in range(size - 1)]
    return lax.ppermute(to_next, axis, up), lax.ppermute(to_prev, axis, down)


def edge_columns(parts):
    rows = jnp.concatenate(parts, axis=0).transpose(1, 0, 2)
    rows = jnp.pad(rows, ((0, 0), (0, EDGE - rows.shape[1]), (0, 0)))
    return rows.reshape(-1, rows.shape[2])


EARLY = 5


def device_work(tokens, grad_output, w_exp, dw_kernel, w_proj, ln_gain, w_qkv, w_out):
    rows, cols, width = tokens.shape
    blocks = w_exp.shape[1] // BLK
    row_count = lax.axis_size("row")
    col_count = lax.axis_size("col")
    groups = [
        [
            (2 * q + h) * col_count + c
            for h in range(2)
            for q in range(row_count // 2)
            for c in range(col_count)
        ]
    ]
    row_at, col_at = lax.axis_index("row"), lax.axis_index("col")
    place = jnp.stack([row_at % 2, row_at // 2 * col_count + col_at]).astype(jnp.int32)

    def exchange(flat):
        sent = flat.reshape(row_count * col_count, -1, flat.shape[1])
        moved = lax.all_to_all(
            sent, ("row", "col"), split_axis=0, concat_axis=0, tiled=True,
            axis_index_groups=groups,
        )
        return moved.reshape(flat.shape)

    from_top, from_bot = neighbour_pair(
        "row",
        row_count,
        jnp.concatenate([tokens[rows - 2 :], grad_output[rows - 1 :]], axis=0),
        jnp.concatenate([tokens[:2], grad_output[:1]], axis=0),
    )
    top, g_top, bot, g_bot = from_top[:2], from_top[2:], from_bot[:2], from_bot[2:]
    grad_flat = grad_output.reshape(rows * cols, width)
    grad_att = grad_att_for_owners(place, grad_flat, w_out)

    near_right = edge_columns([x[:, cols - 2 :] for x in (top, tokens, bot)])
    near_left = edge_columns([x[:, :2] for x in (top, tokens, bot)])
    grad_right = edge_columns([x[:, cols - 1 :] for x in (g_top, grad_output, g_bot)])
    grad_left = edge_columns([x[:, :1] for x in (g_top, grad_output, g_bot)])
    to_right = jnp.concatenate([near_right, grad_right], axis=0)
    to_left = jnp.concatenate([near_left, grad_left], axis=0)
    to_right, to_left, grad_att = lax.optimization_barrier((to_right, to_left, grad_att))
    from_left, from_right = neighbour_pair("col", col_count, to_right, to_left)
    grad_win = exchange(grad_att)

    hidden, sent = forward(
        place, from_top, tokens, from_bot, from_left, from_right, w_exp, dw_kernel, w_proj
    )
    sent, grad_win = lax.optimization_barrier((sent, grad_win))
    hidden_win = exchange(sent)
    w_late, _ = lax.optimization_barrier((w_exp, sent))
    halo = (from_top, tokens, from_bot, from_left, near_left, near_right, from_right)
    tables = slopes(*halo, w_late, dw_kernel, 0, EARLY)
    hidden_win, *tables = lax.optimization_barrier((hidden_win, *tables))
    back_win, att_win = attend(place, hidden_win, grad_win, ln_gain.reshape(1, width), w_qkv)
    back = exchange(back_win)
    w_last, att_win = lax.optimization_barrier((w_exp, att_win))
    tables = slopes(*halo, w_last, dw_kernel, EARLY, blocks - EARLY, tables)
    attn_win = jnp.dot(att_win, w_out, preferred_element_type=jnp.float32).astype(jnp.bfloat16)
    back, attn_win, *tables = lax.optimization_barrier((back, attn_win, *tables))
    attn = exchange(attn_win)
    grad_tokens = backward(
        place, from_top, grad_flat, back, from_bot, from_left, from_right, tables,
        w_exp, dw_kernel, w_proj,
    )
    attn, grad_tokens = lax.optimization_barrier((attn, grad_tokens))
    output = finish(place, hidden, attn)
    return output.reshape(tokens.shape), grad_tokens.reshape(tokens.shape)


def solution(mesh):
    in_specs = (P("row", "col", None), P("row", "col", None), P(), P(), P(), P(), P(), P())
    out_specs = (P("row", "col", None), P("row", "col", None))
    return jax.shard_map(
        device_work, mesh=mesh, in_specs=in_specs, out_specs=out_specs, check_vma=False
    )
```
